256 devices in a mesh: dom: 32 (over x, y, core), tm: 8 (over z).
Axes of the slice: x: 4, y: 4, z: 8, core: 2. Of those that a mesh axis runs over, the one named last changes fastest.
Arguments:
- features: bfloat16 [8, 8192, 512], P('tm', 'dom'), may hold values from -6 to 6
- tile_rows: int32 [8, 768], P('tm', 'dom'), may hold values from 0 to 63, as said below
- tile_cols: int32 [8, 768], P('tm', 'dom'), may hold values from 0 to 63, as said below
- tile_vals: bfloat16 [8, 768, 128, 128], P('tm', 'dom'), may hold values from 0 to 0.0625
- tile_used: int32 [8, 32], P('tm', 'dom'), may hold values from 12 to 24, as said below
- pool_weight: bfloat16 [512, 512], replicated, may hold values from -0.25 to 0.25
- w_in: bfloat16 [3, 512, 512], replicated, may hold values from -0.25 to 0.25
- w_state: bfloat16 [3, 512, 512], replicated, may hold values from -0.25 to 0.25
- gate_offset: float32 [512], replicated, may hold values from 0 to 5
- start_weight: float32 [512, 512], replicated, may hold values from -3 to 3
Outputs:
- hidden_out: bfloat16 [8, 8192, 512], P('tm', 'dom')
- weights_out: float32 [8, 512, 512], P('tm')
The draws below stay inside these ranges and needn't reach their ends.
Inputs may be any that keep to these rules, and one draw needn't show every extreme that they name: `tile_rows`: every slot of row partition d names a row block of that partition, d * 2 to (d + 1) * 2 - 1. `tile_cols`: within one snapshot and one row partition, all slots whose column blocks lie on the same dom index name the same column block. `tile_used`: in every snapshot some row partition has all 24 slots live.
All inputs are finite; a program needn't handle non-finite values.
Results may differ from the reference program's by a relative error of at most 0.017.
Values may be sent and summed in bfloat16 or wider, within the bound.
No kernel may reach another device: no remote copies, remote signals or barrier semaphores. Data moves between devices by JAX's collectives and lax.ppermute only.
A program may use at most 64 MiB of HBM per device.

```python
import jax
import jax.numpy as jnp
from jax import lax

D = 512
BLOCK = 128
TILES_DEV = 24
RB_DEV = 2
NODES = 8192
SNAPS = 8
SLOTS = 768
N_DOM = 32


def draw_tile_rows(key, part):
    offsets = jax.random.randint(key, (SNAPS, N_DOM, TILES_DEV), 0, RB_DEV)
    row_base = (jnp.arange(N_DOM, dtype=jnp.int32) * RB_DEV)[None, :, None]
    return (offsets + row_base).reshape(SNAPS, N_DOM * TILES_DEV).astype(jnp.int32)


def draw_tile_cols(key, part):
    pick_key, peer_key = jax.random.split(key)
    block_picks = jax.random.randint(pick_key, (SNAPS, N_DOM, N_DOM), 0, RB_DEV)
    peer_draw = jax.random.randint(peer_key, (SNAPS, N_DOM, TILES_DEV), 0, N_DOM)
    chosen = jnp.take_along_axis(block_picks, peer_draw, axis=2)
    return (peer_draw * RB_DEV + chosen).reshape(SNAPS, N_DOM * TILES_DEV).astype(jnp.int32)


def draw_tile_used(key, part):
    count_key, full_key = jax.random.split(key)
    counts = jax.random.randint(count_key, (SNAPS, N_DOM), TILES_DEV // 2, TILES_DEV + 1)
    full_at = jax.random.randint(full_key, (SNAPS,), 0, N_DOM)
    positions = jnp.arange(N_DOM, dtype=jnp.int32)[None, :]
    return jnp.where(positions == full_at[:, None], TILES_DEV, counts).astype(jnp.int32)


def steps_of(own_key, extent, pieces, smallest, largest):
    gain = 1.0
    for dim, shards_of in pieces:
        steps = jax.random.uniform(jax.random.fold_in(jax.random.fold_in(own_key, 6), dim), (shards_of,), jnp.float32, smallest / len(pieces), largest / len(pieces))
        gain = gain * jnp.repeat(jnp.exp(steps), extent[dim] // shards_of).reshape((-1,) + (1,) * (len(extent) - 1 - dim))
    return gain


def scatter_about(rng, dims, spread, bound, cuts=(), kind=jnp.bfloat16):
    values = jax.random.normal(rng, dims, jnp.float32) * spread
    if len(cuts) > 0:
        values = steps_of(rng, dims, cuts, -0.22, 0.18) * values
    return jnp.clip(values, min=-bound, max=bound).astype(kind)


def setup_inputs(seed: int = 0) -> dict:
    splits = jax.random.split(jax.random.key(seed), 11)
    return {
        "features": scatter_about(splits[0], (SNAPS, NODES, D), 1.0, 6.0, ((0, 8), (1, 32))),
        "tile_rows": draw_tile_rows(jax.random.fold_in(splits[10], 71), 0),
        "tile_cols": draw_tile_cols(jax.random.fold_in(splits[10], 71), 0),
        "tile_vals": jnp.clip(0.0625 * jax.random.uniform(splits[3], (SNAPS, SLOTS, BLOCK, BLOCK), jnp.float32) ** steps_of(splits[3], (SNAPS, SLOTS, BLOCK, BLOCK), ((0, 8), (1, 32)), -0.2, 0.2), 0.0, 0.0625).astype(jnp.bfloat16),
        "tile_used": draw_tile_used(jax.random.fold_in(splits[10], 71), 0),
        "pool_weight": scatter_about(splits[5], (D, D), D ** -0.5, 0.25),
        "w_in": scatter_about(splits[6], (3, D, D), D ** -0.5, 0.25),
        "w_state": scatter_about(splits[7], (3, D, D), D ** -0.5, 0.25),
        "gate_offset": jnp.clip(jax.random.uniform(splits[8], (D,), jnp.float32, 0.0, 5.0), 0.0, 5.0),
        "start_weight": scatter_about(splits[9], (D, D), 0.5, 3.0, (), jnp.float32),
    }


def gru_step(state, inputs_t, w_state, gate_offset):
    state_b = state.astype(jnp.bfloat16)
    upd_pre = jnp.dot(w_state[0], state_b, preferred_element_type=jnp.float32)
    rst_pre = jnp.dot(w_state[1], state_b, preferred_element_type=jnp.float32)
    update = jax.nn.sigmoid(inputs_t[0] + upd_pre - gate_offset[:, None])
    reset = jax.nn.sigmoid(inputs_t[1] + rst_pre)
    reset_state = (reset * state).astype(jnp.bfloat16)
    candidate = jnp.tanh(inputs_t[2] + jnp.dot(w_state[2], reset_state, preferred_element_type=jnp.float32))
    return (1.0 - update) * state + update * candidate


def reference(features, tile_rows, tile_cols, tile_vals, tile_used, pool_weight, w_in, w_state, gate_offset, start_weight):
    num_blocks = NODES // BLOCK

    def aggregate(inputs):
        snap_feats, rows_blk, cols_blk, tile_block, live_count = inputs
        blocks = snap_feats.reshape(num_blocks, BLOCK, D)
        source = jnp.take(blocks, cols_blk.astype(jnp.int32), axis=0).astype(jnp.float32)
        product = jnp.einsum("jab,jbd->jad", tile_block.astype(jnp.float32), source)
        slot_ids = jnp.arange(N_DOM * TILES_DEV, dtype=jnp.int32)
        valid_mask = (slot_ids % TILES_DEV) < live_count[slot_ids // TILES_DEV]
        product = product * valid_mask.astype(jnp.float32)[:, None, None]
        summed = jax.ops.segment_sum(product, rows_blk.astype(jnp.int32), num_segments=num_blocks)
        return (snap_feats.astype(jnp.float32) + summed.reshape(NODES, D)).astype(jnp.bfloat16)

    aggregated = lax.map(aggregate, (features, tile_rows, tile_cols, tile_vals, tile_used))

    def summarize(snap_feats):
        pool_gates = jax.nn.sigmoid(jnp.dot(snap_feats, pool_weight, preferred_element_type=jnp.float32)).astype(jnp.bfloat16)
        pooled = jnp.dot(snap_feats.T, pool_gates, preferred_element_type=jnp.float32)
        return (pooled * NODES ** -0.5).astype(jnp.bfloat16)

    summary = lax.map(summarize, features)
    in_side = jnp.einsum("gij,tjk->tgik", w_in.astype(jnp.float32), summary.astype(jnp.float32))

    def chain(state, inputs_t):
        new_state = gru_step(state, inputs_t, w_state, gate_offset)
        return new_state, new_state

    final_state, weights_out = lax.scan(chain, start_weight, in_side)

    def project(inputs):
        agg_rows, weight_t = inputs
        mixed = jnp.dot(agg_rows, weight_t.astype(jnp.bfloat16), preferred_element_type=jnp.float32)
        return jnp.maximum(mixed * D ** -0.5, 0.0).astype(jnp.bfloat16)

    hidden_out = lax.map(project, (aggregated, weights_out))
    return hidden_out, weights_out
```

```python
import functools

import jax
import jax.numpy as jnp
from jax import lax
from jax.experimental import pallas as pl
from jax.experimental.pallas import tpu as pltpu
from jax.sharding import Mesh, PartitionSpec as P

BLOCK = 128
X, Y, C = 4, 4, 2
CHIPS = X * Y
F32 = jnp.float32
BF16 = jnp.bfloat16
VM = pltpu.MemorySpace.VMEM
SM = pltpu.MemorySpace.SMEM
NN = (((1,), (0,)), ((), ()))
NT = (((1,), (1,)), ((), ()))
TN = (((0,), (0,)), ((), ()))


def mm(a, b, dims):
    return lax.dot_general(a, b, dims, preferred_element_type=F32)


def vspec():
    return pl.BlockSpec(memory_space=VM)


def sspec():
    return pl.BlockSpec(memory_space=SM)


def call(kernel, out_shape, in_specs, scratch=(), flops=10**8, bytes_accessed=10**6, name=None):
    many = isinstance(out_shape, (tuple, list))
    return pl.pallas_call(
        kernel,
        out_shape=out_shape,
        in_specs=in_specs,
        out_specs=tuple(vspec() for _ in out_shape) if many else vspec(),
        scratch_shapes=list(scratch),
        cost_estimate=pl.CostEstimate(flops=flops, bytes_accessed=bytes_accessed, transcendentals=0),
        name=name,
    )


def pool_send_kernel(core_ref, feat_ref, pool_ref, send_ref):
    half = send_ref.shape[0]
    other = pl.multiple_of((1 - core_ref[0]) * half, half)
    gates = jax.nn.sigmoid(mm(feat_ref[...], pool_ref[:, pl.ds(other, half)], NN)).astype(BF16)
    send_ref[...] = mm(gates, feat_ref[...], TN).astype(BF16)


def pool_keep_kernel(core_ref, feat_ref, pool_ref, keep_ref):
    half = keep_ref.shape[0]
    own = pl.multiple_of(core_ref[0] * half, half)
    gates = jax.nn.sigmoid(mm(feat_ref[...], pool_ref[:, pl.ds(own, half)], NN)).astype(BF16)
    keep_ref[...] = mm(gates, feat_ref[...], TN)


def chain_kernel(meta_ref, summ_ref, w_in_ref, w_state_ref, offset_ref, start_ref, out_ref, side_ref, startt_ref):
    n_t, cols, width = summ_ref.shape
    summ = summ_ref[...].reshape(n_t * cols, width)
    for g in range(3):
        side = mm(summ, w_in_ref[g], NT)
        if g == 0:
            side = side - offset_ref[...]
        side_ref[g] = side.reshape(n_t, cols, width)
    startt_ref[...] = start_ref[...].T
    col0 = pl.multiple_of(meta_ref[1], cols)
    state = startt_ref[pl.ds(col0, cols), :]
    last = meta_ref[0]

    def step(t, state):
        state_b = state.astype(BF16)
        update = jax.nn.sigmoid(side_ref[0, t] + mm(state_b, w_state_ref[0], NT))
        reset = jax.nn.sigmoid(side_ref[1, t] + mm(state_b, w_state_ref[1], NT))
        cand = jnp.tanh(side_ref[2, t] + mm((reset * state).astype(BF16), w_state_ref[2], NT))
        return (1.0 - update) * state + update * cand

    state = lax.fori_loop(0, last + 1, step, state)
    out_ref[...] = jnp.broadcast_to(state.astype(BF16)[None], out_ref.shape)


def agg_kernel(own_idx, oth_idx, tiles_own, tiles_oth, feat_own, feat_oth, blocks, agg_own, agg_oth, rhs, lhs, sems):
    slots = tiles_own.shape[0]
    copies = []
    for p, idx in enumerate((own_idx, oth_idx)):
        for j in range(slots):
            cp = pltpu.make_async_copy(
                blocks.at[idx[0, j]],
                rhs.at[p, pl.ds(j * BLOCK, BLOCK), :],
                sems.at[p * slots + j],
            )
            cp.start()
            copies.append(cp)
    for p, (idx, tiles, feat, out) in enumerate(
        ((own_idx, tiles_own, feat_own, agg_own), (oth_idx, tiles_oth, feat_oth, agg_oth))
    ):
        for j in range(slots):
            tile = tiles[j]
            for r in range(2):
                on = idx[1, j] == r
                lhs[p, r * BLOCK : (r + 1) * BLOCK, j * BLOCK : (j + 1) * BLOCK] = jnp.where(
                    on, tile, jnp.zeros_like(tile)
                )
    for p, (feat, out) in enumerate(((feat_own, agg_own), (feat_oth, agg_oth))):
        for j in range(slots):
            copies[p * slots + j].wait()
        total = mm(lhs[p], rhs[p], NN)
        out[...] = (feat[...].astype(F32) + total).astype(BF16)


def final_kernel(core_ref, wt_own, wt_oth, agg_own, agg_oth, hid_ref, w_ref, wt, agg):
    half = wt_own.shape[0]
    own = pl.multiple_of(core_ref[0] * half, half)
    oth = pl.multiple_of((1 - core_ref[0]) * half, half)
    wt[pl.ds(own, half), :] = wt_own[...]
    wt[pl.ds(oth, half), :] = wt_oth[...]
    agg[:, pl.ds(own, half)] = agg_own[...]
    agg[:, pl.ds(oth, half)] = agg_oth[...]
    width = wt.shape[0]
    mixed = mm(agg[...], wt[...], NT)
    hid_ref[...] = jnp.maximum(mixed * width ** (-0.5), 0.0).astype(BF16)
    w_ref[...] = wt[...].astype(F32).T


def swap(x):
    return lax.ppermute(x, "c", [(0, 1), (1, 0)])


def shards(
    features,
    tile_rows,
    tile_cols,
    tile_vals,
    tile_used,
    pool_weight,
    w_in,
    w_state,
    gate_offset,
    start_weight,
):
    rows_dev, width = features.shape[1:]
    slots = tile_rows.shape[1]
    half = width // 2
    n_tm = lax.axis_size("z")
    core = lax.axis_index("c").astype(jnp.int32)
    chip = (lax.axis_index("x") * Y + lax.axis_index("y")).astype(jnp.int32)
    dom = chip * C + core
    t_index = lax.axis_index("z").astype(jnp.int32)
    core_s = core.reshape(1)
    feat = features[0]
    blocks_dev = rows_dev // BLOCK

    bf_half = jax.ShapeDtypeStruct((half, width), BF16)
    send = call(pool_send_kernel, bf_half, [sspec(), vspec(), vspec()], name="pool_send")(core_s, feat, pool_weight)
    keep = call(
        pool_keep_kernel, jax.ShapeDtypeStruct((half, width), F32), [sspec(), vspec(), vspec()], name="pool_keep"
    )(core_s, feat, pool_weight)
    partial = (keep + swap(send).astype(F32)).astype(BF16)
    cols = half // CHIPS
    parts = lax.all_to_all(partial.reshape(CHIPS, cols, width), ("x", "y"), split_axis=0, concat_axis=0, tiled=True)
    summ = (jnp.sum(parts.astype(F32), axis=0) * (rows_dev * CHIPS * C) ** (-0.5)).astype(BF16)
    summ = lax.all_to_all(
        jnp.broadcast_to(summ[None], (n_tm, cols, width)), "z", split_axis=0, concat_axis=0, tiled=True
    )

    feat_mine = lax.dynamic_slice_in_dim(feat, core * half, half, 1)
    feat_send = lax.dynamic_slice_in_dim(feat, (1 - core) * half, half, 1)
    feat_oth = swap(feat_send)
    chip_blocks = jnp.concatenate([feat_mine, feat_oth]).reshape(1, C * blocks_dev, BLOCK, half)
    spread = jnp.broadcast_to(chip_blocks, (CHIPS, C * blocks_dev, BLOCK, half))
    gathered = lax.all_to_all(spread, ("x", "y"), split_axis=0, concat_axis=0, tiled=True)
    gathered = gathered.reshape(CHIPS * C * blocks_dev, BLOCK, half)

    owner = tile_cols[0] // blocks_dev
    live = jnp.arange(slots, dtype=jnp.int32) < tile_used[0, 0]
    where_to = jnp.where(live, tile_rows[0] - dom * blocks_dev, blocks_dev)
    own_idx = jnp.stack([tile_cols[0], where_to])
    oth_idx = swap(own_idx)

    def place(idx):
        owner = idx[0] // blocks_dev
        flip = (owner % C) ^ core
        return jnp.stack([((owner // C) * C + flip) * blocks_dev + idx[0] % blocks_dev, idx[1]])

    tiles_own = tile_vals[0]
    tiles_oth = swap(tiles_own)
    agg_shape = jax.ShapeDtypeStruct((rows_dev, half), BF16)
    agg_own, agg_send = call(
        agg_kernel,
        (agg_shape, agg_shape),
        [sspec(), sspec(), vspec(), vspec(), vspec(), vspec(), pl.BlockSpec(memory_space=pl.ANY)],
        scratch=[
            pltpu.VMEM((2, slots * BLOCK, half), BF16),
            pltpu.VMEM((2, rows_dev, slots * BLOCK), BF16),
            pltpu.SemaphoreType.DMA((2 * slots,)),
        ],
        name="aggregate",
    )(place(own_idx), place(oth_idx), tiles_own, tiles_oth, feat_mine, feat_oth, gathered)
    agg_oth = swap(agg_send)

    col0 = core * half + chip * cols
    lane0 = col0 // BLOCK
    start_cols = lax.dynamic_slice_in_dim(start_weight, lane0 * BLOCK, BLOCK, 1)
    meta = jnp.stack([t_index, col0 % BLOCK])
    evolved = call(
        chain_kernel,
        jax.ShapeDtypeStruct((CHIPS, cols, width), BF16),
        [sspec(), vspec(), vspec(), vspec(), vspec(), vspec()],
        scratch=[pltpu.VMEM((3, n_tm, cols, width), F32), pltpu.VMEM((BLOCK, width), F32)],
        name="chain",
    )(meta, summ, w_in, w_state, gate_offset[None, :], start_cols)
    wt_own = lax.all_to_all(evolved, ("x", "y"), split_axis=0, concat_axis=0, tiled=True).reshape(half, width)
    wt_oth = swap(wt_own)
    hidden, weights = call(
        final_kernel,
        (jax.ShapeDtypeStruct((rows_dev, width), BF16), jax.ShapeDtypeStruct((width, width), F32)),
        [sspec(), vspec(), vspec(), vspec(), vspec()],
        scratch=[pltpu.VMEM((width, width), BF16), pltpu.VMEM((rows_dev, width), BF16)],
        name="final",
    )(core_s, wt_own, wt_oth, agg_own, agg_oth)
    return hidden[None], weights[None]


def solution(mesh):
    n_tm = mesh.shape["tm"]
    fine = Mesh(mesh.devices.reshape(X, Y, C, n_tm), ("x", "y", "c", "z"))
    dom = ("x", "y", "c")
    in_specs = (
        P("z", dom, None),
        P("z", dom),
        P("z", dom),
        P("z", dom, None, None),
        P("z", dom),
        P(),
        P(),
        P(),
        P(),
        P(),
    )
    out_specs = (P("z", dom, None), P("z", None, None))
    return jax.shard_map(shards, mesh=fine, in_specs=in_specs, out_specs=out_specs, check_vma=False)
```

```python
import jax
import jax.numpy as jnp
from jax import lax
from jax.experimental import pallas as pl
from jax.experimental.pallas import tpu as pltpu
from jax.sharding import Mesh, PartitionSpec as P


BLOCK = 128
X, Y, C = 4, 4, 2
CHIPS = X * Y
F32 = jnp.float32
BF16 = jnp.bfloat16
VM = pltpu.MemorySpace.VMEM
SM = pltpu.MemorySpace.SMEM
NN = (((1,), (0,)), ((), ()))
NT = (((1,), (1,)), ((), ()))
TN = (((0,), (0,)), ((), ()))


def mm(a, b, dims):
    return lax.dot_general(a, b, dims, preferred_element_type=F32)


def vspec():
    return pl.BlockSpec(memory_space=VM)


def sspec():
    return pl.BlockSpec(memory_space=SM)


def call(kernel, out_shape, in_specs, scratch=(), flops=10**8, bytes_accessed=10**6, vmem_mib=8):
    many = isinstance(out_shape, (tuple, list))
    return pl.pallas_call(
        kernel,
        out_shape=out_shape,
        in_specs=in_specs,
        out_specs=tuple(vspec() for _ in out_shape) if many else vspec(),
        scratch_shapes=list(scratch),
        cost_estimate=pl.CostEstimate(flops=flops, bytes_accessed=bytes_accessed, transcendentals=0),
        compiler_params=pltpu.CompilerParams(vmem_limit_bytes=vmem_mib * 2**20),
    )


def pool_send_kernel(core_ref, feat_ref, pool_ref, send_ref):
    half = send_ref.shape[0]
    other = pl.multiple_of((1 - core_ref[0]) * half, half)
    gates = jax.nn.sigmoid(mm(feat_ref[...], pool_ref[:, pl.ds(other, half)], NN)).astype(BF16)
    send_ref[...] = mm(gates, feat_ref[...], TN).astype(BF16)


def pool_keep_kernel(core_ref, feat_ref, pool_ref, keep_ref):
    half = keep_ref.shape[0]
    own = pl.multiple_of(core_ref[0] * half, half)
    gates = jax.nn.sigmoid(mm(feat_ref[...], pool_ref[:, pl.ds(own, half)], NN)).astype(BF16)
    keep_ref[...] = mm(gates, feat_ref[...], TN)


def chain_kernel(meta_ref, summ_ref, w_in_ref, w_state_ref, offset_ref, start_ref, out_ref, side_ref, startt_ref):
    n_t, cols, width = summ_ref.shape
    summ = summ_ref[...].reshape(n_t * cols, width)
    for g in range(3):
        side = mm(summ, w_in_ref[g], NT)
        if g == 0:
            side = side - offset_ref[...]
        side_ref[g] = side.reshape(n_t, cols, width)
    startt_ref[...] = start_ref[...].T
    col0 = pl.multiple_of(meta_ref[1], cols)
    state = startt_ref[pl.ds(col0, cols), :]
    last = meta_ref[0]

    def step(t, state):
        state_b = state.astype(BF16)
        update = jax.nn.sigmoid(side_ref[0, t] + mm(state_b, w_state_ref[0], NT))
        reset = jax.nn.sigmoid(side_ref[1, t] + mm(state_b, w_state_ref[1], NT))
        cand = jnp.tanh(side_ref[2, t] + mm((reset * state).astype(BF16), w_state_ref[2], NT))
        return (1.0 - update) * state + update * cand

    state = lax.fori_loop(0, last + 1, step, state)
    out_ref[...] = jnp.broadcast_to(state.astype(BF16)[None], out_ref.shape)


def agg_kernel(own_idx, oth_idx, tiles_own, tiles_oth, feat_own, feat_oth, *refs):
    pieces, (agg_own, agg_oth, blocks, rhs, lhs, sems) = refs[:-6], refs[-6:]
    slots = tiles_own.shape[0]
    copies = []
    first = 0
    for n, piece in enumerate(pieces):
        cp = pltpu.make_async_copy(piece, blocks.at[pl.ds(first, piece.shape[0])], sems.at[n])
        cp.start()
        copies.append(cp)
        first += piece.shape[0]
    for p, (idx, tiles, feat, out) in enumerate(
        ((own_idx, tiles_own, feat_own, agg_own), (oth_idx, tiles_oth, feat_oth, agg_oth))
    ):
        for j in range(slots):
            tile = tiles[j]
            for r in range(2):
                on = idx[1, j] == r
                lhs[p, r * BLOCK : (r + 1) * BLOCK, j * BLOCK : (j + 1) * BLOCK] = jnp.where(
                    on, tile, jnp.zeros_like(tile)
                )
    for cp in copies:
        cp.wait()
    for p, (idx, feat, out) in enumerate(((own_idx, feat_own, agg_own), (oth_idx, feat_oth, agg_oth))):
        for j in range(slots):
            rhs[p, j * BLOCK : (j + 1) * BLOCK, :] = blocks[idx[0, j]]
        total = mm(lhs[p], rhs[p], NN)
        out[...] = (feat[...].astype(F32) + total).astype(BF16)


def final_kernel(core_ref, wt_own, wt_oth, agg_own, agg_oth, hid_ref, w_ref, wt, agg):
    half = wt_own.shape[0]
    own = pl.multiple_of(core_ref[0] * half, half)
    oth = pl.multiple_of((1 - core_ref[0]) * half, half)
    wt[pl.ds(own, half), :] = wt_own[...]
    wt[pl.ds(oth, half), :] = wt_oth[...]
    agg[:, pl.ds(own, half)] = agg_own[...]
    agg[:, pl.ds(oth, half)] = agg_oth[...]
    width = wt.shape[0]
    mixed = mm(agg[...], wt[...], NT)
    hid_ref[...] = jnp.maximum(mixed * width ** (-0.5), 0.0).astype(BF16)
    w_ref[...] = wt[...].astype(F32).T


def swap(x):
    return lax.ppermute(x, "c", [(0, 1), (1, 0)])


def trade(x, axes):
    return lax.all_to_all(x, axes, split_axis=0, concat_axis=0, tiled=True)


def shift(x, axis, distance):
    size = lax.axis_size(axis)
    return lax.ppermute(x, axis, [(i, (i + distance) % size) for i in range(size)])


def spread(x, axis):
    below = shift(x, axis, 1)
    above = shift(x, axis, -1)
    part = x.shape[0] // 2
    low = shift(below[:part], axis, 1)
    high = shift(above[part:], axis, -1)
    return [x, below, above, low, high]


def slot_of(there, here):
    step = (there - here) % 4
    return jnp.where(step == 0, 0, jnp.where(step == 3, 1, step + 1))


def layer(
    features,
    tile_rows,
    tile_cols,
    tile_vals,
    tile_used,
    pool_weight,
    w_in,
    w_state,
    gate_offset,
    start_weight,
):
    rows_dev, width = features.shape[1:]
    slots = tile_rows.shape[1]
    half = width // 2
    n_tm = lax.axis_size("z")
    core = lax.axis_index("c").astype(jnp.int32)
    chip = (lax.axis_index("x") * Y + lax.axis_index("y")).astype(jnp.int32)
    dom = chip * C + core
    t_index = lax.axis_index("z").astype(jnp.int32)
    core_s = core.reshape(1)
    feat = features[0]
    blocks_dev = rows_dev // BLOCK

    bf_half = jax.ShapeDtypeStruct((half, width), BF16)
    send = call(pool_send_kernel, bf_half, [sspec(), vspec(), vspec()])(core_s, feat, pool_weight)
    keep = call(
        pool_keep_kernel, jax.ShapeDtypeStruct((half, width), F32), [sspec(), vspec(), vspec()]
    )(core_s, feat, pool_weight)
    partial = (keep + swap(send).astype(F32)).astype(BF16)
    cols = half // CHIPS
    parts = trade(partial.reshape(CHIPS, cols, width), ("x", "y"))
    summ = (jnp.sum(parts.astype(F32), axis=0) * (rows_dev * CHIPS * C) ** (-0.5)).astype(BF16)
    summ = trade(jnp.broadcast_to(summ[None], (n_tm, cols, width)), "z")

    feat_mine = lax.dynamic_slice_in_dim(feat, core * half, half, 1)
    feat_send = lax.dynamic_slice_in_dim(feat, (1 - core) * half, half, 1)
    feat_oth = swap(feat_send)
    blocks_a = spread(feat_mine.reshape(blocks_dev, BLOCK, half), "x")
    blocks_b = spread(feat_oth.reshape(blocks_dev, BLOCK, half), "y")
    blocks_a = spread(jnp.concatenate(blocks_a), "y")
    blocks_b = spread(jnp.concatenate(blocks_b), "x")
    gathered = blocks_a + blocks_b

    live = jnp.arange(slots, dtype=jnp.int32) < tile_used[0, 0]
    where_to = jnp.where(live, tile_rows[0] - dom * blocks_dev, blocks_dev)
    own_idx = jnp.stack([tile_cols[0], where_to])
    oth_idx = swap(own_idx)

    def place(idx):
        owner, block = idx[0] // blocks_dev, idx[0] % blocks_dev
        in_x = slot_of(owner // (Y * C), lax.axis_index("x"))
        in_y = slot_of((owner // C) % Y, lax.axis_index("y"))
        in_a = (in_y * 4 + in_x) * blocks_dev + block
        in_b = (in_x * 4 + in_y) * blocks_dev + block + CHIPS * blocks_dev
        return jnp.stack([jnp.where(owner % C == core, in_a, in_b), idx[1]])

    tiles_own = tile_vals[0]
    tiles_oth = swap(tiles_own)
    agg_shape = jax.ShapeDtypeStruct((rows_dev, half), BF16)
    agg_own, agg_send = call(
        agg_kernel,
        (agg_shape, agg_shape),
        [sspec(), sspec(), vspec(), vspec(), vspec(), vspec()] + [pl.BlockSpec(memory_space=pl.ANY)] * len(gathered),
        scratch=[
            pltpu.VMEM((CHIPS * C * blocks_dev, BLOCK, half), BF16),
            pltpu.VMEM((2, slots * BLOCK, half), BF16),
            pltpu.VMEM((2, rows_dev, slots * BLOCK), BF16),
            pltpu.SemaphoreType.DMA((len(gathered),)),
        ],
        vmem_mib=20,
    )(place(own_idx), place(oth_idx), tiles_own, tiles_oth, feat_mine, feat_oth, *gathered)
    agg_oth = swap(agg_send)

    col0 = core * half + chip * cols
    lane0 = col0 // BLOCK
    start_cols = lax.dynamic_slice_in_dim(start_weight, lane0 * BLOCK, BLOCK, 1)
    meta = jnp.stack([t_index, col0 % BLOCK])
    evolved = call(
        chain_kernel,
        jax.ShapeDtypeStruct((CHIPS, cols, width), BF16),
        [sspec(), vspec(), vspec(), vspec(), vspec(), vspec()],
        scratch=[pltpu.VMEM((3, n_tm, cols, width), F32), pltpu.VMEM((BLOCK, width), F32)],
        vmem_mib=12,
    )(meta, summ, w_in, w_state, gate_offset[None, :], start_cols)
    wt_own = trade(evolved, ("x", "y")).reshape(half, width)
    wt_oth = swap(wt_own)
    hidden, weights = call(
        final_kernel,
        (jax.ShapeDtypeStruct((rows_dev, width), BF16), jax.ShapeDtypeStruct((width, width), F32)),
        [sspec(), vspec(), vspec(), vspec(), vspec()],
        scratch=[pltpu.VMEM((width, width), BF16), pltpu.VMEM((rows_dev, width), BF16)],
    )(core_s, wt_own, wt_oth, agg_own, agg_oth)
    return hidden[None], weights[None]


def solution(mesh):
    n_tm = mesh.shape["tm"]
    fine = Mesh(mesh.devices.reshape(X, Y, C, n_tm), ("x", "y", "c", "z"))
    dom = ("x", "y", "c")
    in_specs = (
        P("z", dom, None),
        P("z", dom),
        P("z", dom),
        P("z", dom, None, None),
        P("z", dom),
        P(),
        P(),
        P(),
        P(),
        P(),
    )
    out_specs = (P("z", dom, None), P("z", None, None))
    return jax.shard_map(layer, mesh=fine, in_specs=in_specs, out_specs=out_specs, check_vma=False)
```

```python
import jax
import jax.numpy as jnp
from jax import lax
from jax.experimental import pallas as pl
from jax.experimental.pallas import tpu as pltpu
from jax.sharding import Mesh, PartitionSpec as P


BLOCK = 128
X, Y, C = 4, 4, 2
CHIPS = X * Y
F32 = jnp.float32
BF16 = jnp.bfloat16
VM = pltpu.MemorySpace.VMEM
SM = pltpu.MemorySpace.SMEM
HB = pltpu.MemorySpace.HBM
NN = (((1,), (0,)), ((), ()))
NT = (((1,), (1,)), ((), ()))
TN = (((0,), (0,)), ((), ()))


def mm(a, b, dims):
    return lax.dot_general(a, b, dims, preferred_element_type=F32)


def vspec():
    return pl.BlockSpec(memory_space=VM)


def hspec():
    return pl.BlockSpec(memory_space=HB)


def sspec():
    return pl.BlockSpec(memory_space=SM)


def call(kernel, out_shape, in_specs, scratch=(), flops=10**8, bytes_accessed=10**6, vmem_mib=8, out=None):
    many = isinstance(out_shape, (tuple, list))
    return pl.pallas_call(
        kernel,
        out_shape=out_shape,
        in_specs=in_specs,
        out_specs=out or (tuple(vspec() for _ in out_shape) if many else vspec()),
        scratch_shapes=list(scratch),
        cost_estimate=pl.CostEstimate(flops=flops, bytes_accessed=bytes_accessed, transcendentals=0),
        compiler_params=pltpu.CompilerParams(vmem_limit_bytes=vmem_mib * 2**20),
    )


def pool_kernel(core_ref, feat_hbm, pool_hbm, send_ref, keep_ref, mine_ref, give_ref, feat_ref, pool_ref, sems):
    fetch = [pltpu.make_async_copy(feat_hbm, feat_ref, sems.at[0]), pltpu.make_async_copy(pool_hbm, pool_ref, sems.at[1])]
    for cp in fetch:
        cp.start()
    for cp in fetch:
        cp.wait()
    half = send_ref.shape[0]
    own = pl.multiple_of(core_ref[0] * half, half)
    other = pl.multiple_of((1 - core_ref[0]) * half, half)
    feat = feat_ref[...]
    gates = jax.nn.sigmoid(mm(feat, pool_ref[:, pl.ds(other, half)], NN)).astype(BF16)
    send_ref[...] = mm(gates, feat, TN).astype(BF16)
    gates = jax.nn.sigmoid(mm(feat, pool_ref[:, pl.ds(own, half)], NN)).astype(BF16)
    keep_ref[...] = mm(gates, feat, TN)
    mine_ref[...] = feat_ref[:, pl.ds(own, half)]
    give_ref[...] = feat_ref[:, pl.ds(other, half)]


def join_kernel(a_ref, b_ref, out_ref):
    n = a_ref.shape[0]
    out_ref[:n] = a_ref[...]
    out_ref[n:] = b_ref[...]


def join(a, b):
    shape = jax.ShapeDtypeStruct((a.shape[0] + b.shape[0],) + a.shape[1:], a.dtype)
    return call(join_kernel, shape, [vspec(), vspec()], flops=0)(a, b)


def chain_kernel(meta_ref, summ_ref, w_in_ref, w_state_ref, offset_ref, start_ref, out_hbm, side_ref, startt_ref, w_ref, out_ref, sems):
    fetch = pltpu.make_async_copy(w_state_ref, w_ref, sems.at[0])
    fetch.start()
    n_t, cols, width = summ_ref.shape
    summ = summ_ref[...].reshape(n_t * cols, width)
    for g in range(3):
        side = mm(summ, w_in_ref[g], NT)
        if g == 0:
            side = side - offset_ref[...]
        side_ref[g] = side.reshape(n_t, cols, width)
    startt_ref[...] = start_ref[...].T
    col0 = pl.multiple_of(meta_ref[1], cols)
    state = startt_ref[pl.ds(col0, cols), :]
    last = meta_ref[0]
    fetch.wait()

    def step(t, state):
        state_b = state.astype(BF16)
        update = jax.nn.sigmoid(side_ref[0, t] + mm(state_b, w_ref[0], NT))
        reset = jax.nn.sigmoid(side_ref[1, t] + mm(state_b, w_ref[1], NT))
        cand = jnp.tanh(side_ref[2, t] + mm((reset * state).astype(BF16), w_ref[2], NT))
        return (1.0 - update) * state + update * cand

    state = lax.fori_loop(0, last + 1, step, state)
    out_ref[...] = jnp.broadcast_to(state.astype(BF16)[None], out_ref.shape)
    store = pltpu.make_async_copy(out_ref, out_hbm, sems.at[1])
    store.start()
    store.wait()


def masked(idx, tiles, lhs):
    for j in range(tiles.shape[0]):
        tile = tiles[j]
        for r in range(2):
            lhs[r * BLOCK : (r + 1) * BLOCK, j * BLOCK : (j + 1) * BLOCK] = jnp.where(
                idx[1, j] == r, tile, jnp.zeros_like(tile)
            )


def slot_of(step):
    return jnp.where(step == 0, 0, jnp.where(step == 3, 1, step + 1))


def agg_oth_kernel(here, own_idx, oth_idx, tiles, feat, *refs):
    pieces, (agg, rhs_own, blocks, rhs, lhs, sems) = refs[:-6], refs[-6:]
    copies = []
    first = 0
    for n, piece in enumerate(pieces):
        cp = pltpu.make_async_copy(piece, blocks.at[pl.ds(first, piece.shape[0])], sems.at[n])
        cp.start()
        copies.append(cp)
        first += piece.shape[0]
    masked(oth_idx, tiles, lhs)
    for cp in copies:
        cp.wait()
    per_dev = first // (CHIPS * C)
    for idx, out in ((oth_idx, rhs), (own_idx, rhs_own)):
        for j in range(tiles.shape[0]):
            col = idx[0, j]
            owner = lax.div(col, per_dev)
            in_x = slot_of((lax.div(owner, Y * C) - here[0]) & 3)
            in_y = slot_of((lax.div(owner, C) - here[1]) & 3)
            same = (owner & 1) == here[2]
            place = jnp.where(same, in_y * 4 + in_x, in_x * 4 + in_y + CHIPS)
            out[j * BLOCK : (j + 1) * BLOCK, :] = blocks[place * per_dev + lax.rem(col, per_dev)]
    agg[...] = (feat[...].astype(F32) + mm(lhs[...], rhs[...], NN)).astype(BF16)


def agg_own_kernel(own_idx, tiles, feat, rhs, agg, lhs):
    masked(own_idx, tiles, lhs)
    agg[...] = (feat[...].astype(F32) + mm(lhs[...], rhs[...], NN)).astype(BF16)


def final_kernel(core_ref, wt_own, wt_oth, agg_own, agg_oth, hid_ref, w_ref, wt, agg):
    half = wt_own.shape[0]
    own = pl.multiple_of(core_ref[0] * half, half)
    oth = pl.multiple_of((1 - core_ref[0]) * half, half)
    wt[pl.ds(own, half), :] = wt_own[...]
    wt[pl.ds(oth, half), :] = wt_oth[...]
    agg[:, pl.ds(own, half)] = agg_own[...]
    agg[:, pl.ds(oth, half)] = agg_oth[...]
    width = wt.shape[0]
    mixed = mm(agg[...], wt[...], NT)
    hid_ref[...] = jnp.maximum(mixed * width ** (-0.5), 0.0).astype(BF16)
    w_ref[...] = wt[...].astype(F32).T


def swap(x):
    return lax.ppermute(x, "c", [(0, 1), (1, 0)])


def trade(x, axes):
    return lax.all_to_all(x, axes, split_axis=0, concat_axis=0, tiled=True)


def shift(x, axis, distance):
    size = lax.axis_size(axis)
    return lax.ppermute(x, axis, [(i, (i + distance) % size) for i in range(size)])


def spread(x, axis):
    below = shift(x, axis, 1)
    above = shift(x, axis, -1)
    return [x, below, above, shift(below, axis, 1)]


def spread2(low, high, axis):
    below = [shift(low, axis, 1), shift(high, axis, 1)]
    above = [shift(low, axis, -1), shift(high, axis, -1)]
    opposite = [shift(below[0], axis, 1), shift(above[1], axis, -1)]
    return [low, high] + below + above + opposite


def layer(
    features,
    tile_rows,
    tile_cols,
    tile_vals,
    tile_used,
    pool_weight,
    w_in,
    w_state,
    gate_offset,
    start_weight,
):
    rows_dev, width = features.shape[1:]
    slots = tile_rows.shape[1]
    half = width // 2
    n_tm = lax.axis_size("z")
    core = lax.axis_index("c").astype(jnp.int32)
    chip = (lax.axis_index("x") * Y + lax.axis_index("y")).astype(jnp.int32)
    dom = chip * C + core
    t_index = lax.axis_index("z").astype(jnp.int32)
    core_s = core.reshape(1)
    feat = features[0]
    blocks_dev = rows_dev // BLOCK

    bf_half = jax.ShapeDtypeStruct((half, width), BF16)
    feat_half = jax.ShapeDtypeStruct((rows_dev, half), BF16)
    send, keep, feat_mine, feat_give = call(
        pool_kernel,
        (bf_half, jax.ShapeDtypeStruct((half, width), F32), feat_half, feat_half),
        [sspec(), hspec(), hspec()],
        scratch=[pltpu.VMEM(feat.shape, BF16), pltpu.VMEM(pool_weight.shape, BF16), pltpu.SemaphoreType.DMA((2,))],
    )(core_s, feat, pool_weight)
    partial = (keep + swap(send).astype(F32)).astype(BF16)
    cols = half // CHIPS
    parts = trade(partial.reshape(CHIPS, cols, width), ("x", "y"))
    summ = (jnp.sum(parts.astype(F32), axis=0) * (rows_dev * CHIPS * C) ** (-0.5)).astype(BF16)
    summ = trade(jnp.broadcast_to(summ[None], (n_tm, cols, width)), "z")

    feat_oth = swap(feat_give)
    four = (blocks_dev, BLOCK, half)
    blocks_a = spread(feat_mine.reshape(four), "x")
    blocks_b = spread(feat_oth.reshape(four), "y")
    low_a, low_b = join(*blocks_a[:2]), join(*blocks_b[:2])
    high_a, high_b = join(*blocks_a[2:]), join(*blocks_b[2:])
    gathered = spread2(low_a, high_a, "y") + spread2(low_b, high_b, "x")

    live = jnp.arange(slots, dtype=jnp.int32) < tile_used[0, 0]
    where_to = jnp.where(live, tile_rows[0] - dom * blocks_dev, blocks_dev)
    own_idx = jnp.stack([tile_cols[0], where_to])
    oth_idx = swap(own_idx)

    tiles_own = tile_vals[0]
    tiles_oth = swap(tiles_own)
    here = jnp.stack([lax.axis_index("x"), lax.axis_index("y"), core]).astype(jnp.int32)
    depth = slots * BLOCK
    lhs = pltpu.VMEM((rows_dev, depth), BF16)
    agg_give, rhs_own = call(
        agg_oth_kernel,
        (feat_half, jax.ShapeDtypeStruct((depth, half), BF16)),
        [sspec()] * 3 + [vspec()] * 2 + [pl.BlockSpec(memory_space=pl.ANY)] * len(gathered),
        scratch=[
            pltpu.VMEM((CHIPS * C * blocks_dev, BLOCK, half), BF16),
            pltpu.VMEM((depth, half), BF16),
            lhs,
            pltpu.SemaphoreType.DMA((len(gathered),)),
        ],
        vmem_mib=16,
    )(here, own_idx, oth_idx, tiles_oth, feat_oth, *gathered)
    agg_oth = swap(agg_give)
    agg_own = call(
        agg_own_kernel, feat_half, [sspec()] + [vspec()] * 3, scratch=[lhs], vmem_mib=8
    )(own_idx, tiles_own, feat_mine, rhs_own)

    col0 = core * half + chip * cols
    lane0 = col0 // BLOCK
    start_cols = lax.dynamic_slice_in_dim(start_weight, lane0 * BLOCK, BLOCK, 1)
    meta = jnp.stack([t_index, col0 % BLOCK])
    evolved = call(
        chain_kernel,
        jax.ShapeDtypeStruct((CHIPS, cols, width), BF16),
        [sspec(), vspec(), vspec(), hspec(), vspec(), vspec()],
        scratch=[
            pltpu.VMEM((3, n_tm, cols, width), F32),
            pltpu.VMEM((BLOCK, width), F32),
            pltpu.VMEM(w_state.shape, BF16),
            pltpu.VMEM((CHIPS, cols, width), BF16),
            pltpu.SemaphoreType.DMA((2,)),
        ],
        out=hspec(),
        vmem_mib=12,
    )(meta, summ, w_in, w_state, gate_offset[None, :], start_cols)
    wt_own = trade(evolved, ("x", "y")).reshape(half, width)
    wt_oth = swap(wt_own)
    hidden, weights = call(
        final_kernel,
        (jax.ShapeDtypeStruct((rows_dev, width), BF16), jax.ShapeDtypeStruct((width, width), F32)),
        [sspec(), vspec(), vspec(), vspec(), vspec()],
        scratch=[pltpu.VMEM((width, width), BF16), pltpu.VMEM((rows_dev, width), BF16)],
    )(core_s, wt_own, wt_oth, agg_own, agg_oth)
    return hidden[None], weights[None]


def solution(mesh):
    n_tm = mesh.shape["tm"]
    fine = Mesh(mesh.devices.reshape(X, Y, C, n_tm), ("x", "y", "c", "z"))
    dom = ("x", "y", "c")
    in_specs = (
        P("z", dom, None),
        P("z", dom),
        P("z", dom),
        P("z", dom, None, None),
        P("z", dom),
        P(),
        P(),
        P(),
        P(),
        P(),
    )
    out_specs = (P("z", dom, None), P("z", None, None))
    return jax.shard_map(layer, mesh=fine, in_specs=in_specs, out_specs=out_specs, check_vma=False)
```

```python
import functools

import jax
import jax.numpy as jnp
from jax import lax
from jax.experimental import pallas as pl
from jax.experimental.pallas import tpu as pltpu
from jax.sharding import Mesh, PartitionSpec as P


BLOCK = 128
X, Y, C = 4, 4, 2
WHOLE = 60
CHIPS = X * Y
F32 = jnp.float32
BF16 = jnp.bfloat16
VM = pltpu.MemorySpace.VMEM
SM = pltpu.MemorySpace.SMEM
HB = pltpu.MemorySpace.HBM
NN = (((1,), (0,)), ((), ()))
NT = (((1,), (1,)), ((), ()))
TN = (((0,), (0,)), ((), ()))


def mm(a, b, dims):
    return lax.dot_general(a, b, dims, preferred_element_type=F32)


def vspec():
    return pl.BlockSpec(memory_space=VM)


def hspec():
    return pl.BlockSpec(memory_space=HB)


def sspec():
    return pl.BlockSpec(memory_space=SM)


def call(kernel, out_shape, in_specs, scratch=(), flops=10**8, bytes_accessed=10**6, vmem_mib=8, out=None):
    many = isinstance(out_shape, (tuple, list))
    return pl.pallas_call(
        kernel,
        out_shape=out_shape,
        in_specs=in_specs,
        out_specs=out or (tuple(vspec() for _ in out_shape) if many else vspec()),
        scratch_shapes=list(scratch),
        cost_estimate=pl.CostEstimate(flops=flops, bytes_accessed=bytes_accessed, transcendentals=0),
        compiler_params=pltpu.CompilerParams(vmem_limit_bytes=vmem_mib * 2**20),
    )


def pool_kernel(core_ref, feat_hbm, pool_hbm, send_ref, keep_ref, mine_ref, give_ref, feat_ref, pool_ref, sems):
    fetch = [pltpu.make_async_copy(feat_hbm, feat_ref, sems.at[0]), pltpu.make_async_copy(pool_hbm, pool_ref, sems.at[1])]
    for cp in fetch:
        cp.start()
    for cp in fetch:
        cp.wait()
    half = send_ref.shape[0]
    own = pl.multiple_of(core_ref[0] * half, half)
    other = pl.multiple_of((1 - core_ref[0]) * half, half)
    feat = feat_ref[...]
    gates = jax.nn.sigmoid(mm(feat, pool_ref[:, pl.ds(other, half)], NN)).astype(BF16)
    send_ref[...] = mm(gates, feat, TN).astype(BF16)
    gates = jax.nn.sigmoid(mm(feat, pool_ref[:, pl.ds(own, half)], NN)).astype(BF16)
    keep_ref[...] = mm(gates, feat, TN)
    mine_ref[...] = feat_ref[:, pl.ds(own, half)]
    give_ref[...] = feat_ref[:, pl.ds(other, half)]


def join_kernel(*refs):
    pieces, (low, high, sems) = refs[:-3], refs[-3:]
    half = len(pieces) // 2
    copies = []
    for n, piece in enumerate(pieces):
        out = low if n < half else high
        size = piece.shape[0]
        cp = pltpu.make_async_copy(piece, out.at[pl.ds((n % half) * size, size)], sems.at[n])
        cp.start()
        copies.append(cp)
    for cp in copies:
        cp.wait()


def join(a, b):
    shape = jax.ShapeDtypeStruct((len(a) * a[0].shape[0],) + a[0].shape[1:], a[0].dtype)
    pieces = a + b
    return call(
        join_kernel,
        (shape, shape),
        [pl.BlockSpec(memory_space=pl.ANY)] * len(pieces),
        scratch=[pltpu.SemaphoreType.DMA((len(pieces),))],
        flops=0,
        vmem_mib=WHOLE,
    )(*pieces)


def sum_kernel(scale, parts_ref, out_ref):
    total = jnp.sum(parts_ref[...].astype(F32), axis=0) * scale
    out_ref[...] = jnp.broadcast_to(total.astype(BF16)[None], out_ref.shape)


def chain_kernel(
    meta_ref, summ_ref, w_in_hbm, w_state_hbm, offset_ref, start_ref, out_hbm, side_ref, startt_ref, w_in_ref, w_ref, out_ref, sems
):
    fetch_in = pltpu.make_async_copy(w_in_hbm, w_in_ref, sems.at[2])
    fetch_in.start()
    fetch = pltpu.make_async_copy(w_state_hbm, w_ref, sems.at[0])
    fetch.start()
    n_t, cols, width = summ_ref.shape
    summ = summ_ref[...].reshape(n_t * cols, width)
    startt_ref[...] = start_ref[...].T
    fetch_in.wait()
    for g in range(3):
        side = mm(summ, w_in_ref[g], NT)
        if g == 0:
            side = side - offset_ref[...]
        side_ref[g] = side.reshape(n_t, cols, width)
    col0 = pl.multiple_of(meta_ref[1], cols)
    state = startt_ref[pl.ds(col0, cols), :]
    last = meta_ref[0]
    fetch.wait()

    def step(t, state):
        state_b = state.astype(BF16)
        update = jax.nn.sigmoid(side_ref[0, t] + mm(state_b, w_ref[0], NT))
        reset = jax.nn.sigmoid(side_ref[1, t] + mm(state_b, w_ref[1], NT))
        cand = jnp.tanh(side_ref[2, t] + mm((reset * state).astype(BF16), w_ref[2], NT))
        return (1.0 - update) * state + update * cand

    state = lax.fori_loop(0, last + 1, step, state)
    out_ref[...] = jnp.broadcast_to(state.astype(BF16)[None], out_ref.shape)
    store = pltpu.make_async_copy(out_ref, out_hbm, sems.at[1])
    store.start()
    store.wait()


def masked(idx, tiles, lhs):
    for j in range(tiles.shape[0]):
        tile = tiles[j]
        for r in range(2):
            lhs[r * BLOCK : (r + 1) * BLOCK, j * BLOCK : (j + 1) * BLOCK] = jnp.where(
                idx[1, j] == r, tile, jnp.zeros_like(tile)
            )


def slot_of(step):
    return jnp.where(step == 0, 0, jnp.where(step == 3, 1, step + 1))


def agg_oth_kernel(here, own_idx, oth_idx, tiles, feat, *refs):
    pieces, (agg, rhs_own, blocks, rhs, lhs, sems) = refs[:-6], refs[-6:]
    copies = []
    first = 0
    for n, piece in enumerate(pieces):
        cp = pltpu.make_async_copy(piece, blocks.at[pl.ds(first, piece.shape[0])], sems.at[n])
        cp.start()
        copies.append(cp)
        first += piece.shape[0]
    masked(oth_idx, tiles, lhs)
    for cp in copies:
        cp.wait()
    per_dev = first // (CHIPS * C)
    for idx, out in ((oth_idx, rhs), (own_idx, rhs_own)):
        for j in range(tiles.shape[0]):
            col = idx[0, j]
            owner = lax.div(col, per_dev)
            in_x = slot_of((lax.div(owner, Y * C) - here[0]) & 3)
            in_y = slot_of((lax.div(owner, C) - here[1]) & 3)
            same = (owner & 1) == here[2]
            place = jnp.where(same, in_y * 4 + in_x, in_x * 4 + in_y + CHIPS)
            out[j * BLOCK : (j + 1) * BLOCK, :] = blocks[place * per_dev + lax.rem(col, per_dev)]
    agg[...] = (feat[...].astype(F32) + mm(lhs[...], rhs[...], NN)).astype(BF16)


def agg_own_kernel(own_idx, tiles, feat, rhs, agg, lhs):
    masked(own_idx, tiles, lhs)
    agg[...] = (feat[...].astype(F32) + mm(lhs[...], rhs[...], NN)).astype(BF16)


def final_kernel(core_ref, wt_own, wt_oth, agg_own, agg_oth, hid_ref, w_ref, wt, agg):
    half = wt_own.shape[0]
    own = pl.multiple_of(core_ref[0] * half, half)
    oth = pl.multiple_of((1 - core_ref[0]) * half, half)
    wt[pl.ds(own, half), :] = wt_own[...]
    wt[pl.ds(oth, half), :] = wt_oth[...]
    agg[:, pl.ds(own, half)] = agg_own[...]
    agg[:, pl.ds(oth, half)] = agg_oth[...]
    width = wt.shape[0]
    mixed = mm(agg[...], wt[...], NT)
    hid_ref[...] = jnp.maximum(mixed * width ** (-0.5), 0.0).astype(BF16)
    w_ref[...] = wt[...].astype(F32).T


def swap(x):
    return lax.ppermute(x, "c", [(0, 1), (1, 0)])


def trade(x, axes):
    return lax.all_to_all(x, axes, split_axis=0, concat_axis=0, tiled=True)


def shift(x, axis, distance):
    size = lax.axis_size(axis)
    return lax.ppermute(x, axis, [(i, (i + distance) % size) for i in range(size)])


def spread(x, axis):
    return [x] + [shift(x, axis, step) for step in (1, -1, 2)]


def layer(
    features,
    tile_rows,
    tile_cols,
    tile_vals,
    tile_used,
    pool_weight,
    w_in,
    w_state,
    gate_offset,
    start_weight,
):
    rows_dev, width = features.shape[1:]
    slots = tile_rows.shape[1]
    half = width // 2
    n_tm = lax.axis_size("z")
    core = lax.axis_index("c").astype(jnp.int32)
    chip = (lax.axis_index("x") * Y + lax.axis_index("y")).astype(jnp.int32)
    dom = chip * C + core
    t_index = lax.axis_index("z").astype(jnp.int32)
    core_s = core.reshape(1)
    feat = features[0]
    blocks_dev = rows_dev // BLOCK

    bf_half = jax.ShapeDtypeStruct((half, width), BF16)
    feat_half = jax.ShapeDtypeStruct((rows_dev, half), BF16)
    send, keep, feat_mine, feat_give = call(
        pool_kernel,
        (bf_half, jax.ShapeDtypeStruct((half, width), F32), feat_half, feat_half),
        [sspec(), hspec(), hspec()],
        scratch=[pltpu.VMEM(feat.shape, BF16), pltpu.VMEM(pool_weight.shape, BF16), pltpu.SemaphoreType.DMA((2,))],
    )(core_s, feat, pool_weight)
    partial = (keep + swap(send).astype(F32)).astype(BF16)
    cols = half // CHIPS
    parts = trade(partial.reshape(CHIPS, cols, width), ("x", "y"))
    snaps = jax.ShapeDtypeStruct((n_tm, cols, width), BF16)
    scale = (rows_dev * CHIPS * C) ** (-0.5)
    summ = call(functools.partial(sum_kernel, scale), snaps, [vspec()], flops=10**7, vmem_mib=WHOLE)(parts)
    summ = trade(summ, "z")

    feat_oth = swap(feat_give)
    four = (blocks_dev, BLOCK, half)
    blocks_a = spread(feat_mine.reshape(four), "x")
    blocks_b = spread(feat_oth.reshape(four), "y")
    joined_a, joined_b = join(blocks_a, blocks_b)
    gathered = spread(joined_a, "y") + spread(joined_b, "x")

    live = jnp.arange(slots, dtype=jnp.int32) < tile_used[0, 0]
    where_to = jnp.where(live, tile_rows[0] - dom * blocks_dev, blocks_dev)
    own_idx = jnp.stack([tile_cols[0], where_to])
    oth_idx = swap(own_idx)

    tiles_own = tile_vals[0]
    tiles_oth = swap(tiles_own)
    here = jnp.stack([lax.axis_index("x"), lax.axis_index("y"), core]).astype(jnp.int32)
    depth = slots * BLOCK
    lhs = pltpu.VMEM((rows_dev, depth), BF16)
    agg_give, rhs_own = call(
        agg_oth_kernel,
        (feat_half, jax.ShapeDtypeStruct((depth, half), BF16)),
        [sspec()] * 3 + [vspec()] * 2 + [pl.BlockSpec(memory_space=pl.ANY)] * len(gathered),
        scratch=[
            pltpu.VMEM((CHIPS * C * blocks_dev, BLOCK, half), BF16),
            pltpu.VMEM((depth, half), BF16),
            lhs,
            pltpu.SemaphoreType.DMA((len(gathered),)),
        ],
        vmem_mib=WHOLE,
    )(here, own_idx, oth_idx, tiles_oth, feat_oth, *gathered)
    agg_oth = swap(agg_give)
    agg_own = call(
        agg_own_kernel, feat_half, [sspec()] + [vspec()] * 3, scratch=[lhs], vmem_mib=8
    )(own_idx, tiles_own, feat_mine, rhs_own)

    col0 = core * half + chip * cols
    lane0 = col0 // BLOCK
    start_cols = lax.dynamic_slice_in_dim(start_weight, lane0 * BLOCK, BLOCK, 1)
    meta = jnp.stack([t_index, col0 % BLOCK])
    evolved = call(
        chain_kernel,
        jax.ShapeDtypeStruct((CHIPS, cols, width), BF16),
        [sspec(), vspec(), hspec(), hspec(), vspec(), vspec()],
        scratch=[
            pltpu.VMEM((3, n_tm, cols, width), F32),
            pltpu.VMEM((BLOCK, width), F32),
            pltpu.VMEM(w_in.shape, BF16),
            pltpu.VMEM(w_state.shape, BF16),
            pltpu.VMEM((CHIPS, cols, width), BF16),
            pltpu.SemaphoreType.DMA((3,)),
        ],
        out=hspec(),
        vmem_mib=WHOLE,
    )(meta, summ, w_in, w_state, gate_offset[None, :], start_cols)
    wt_own = trade(evolved, ("x", "y")).reshape(half, width)
    wt_oth = swap(wt_own)
    hidden, weights = call(
        final_kernel,
        (jax.ShapeDtypeStruct((rows_dev, width), BF16), jax.ShapeDtypeStruct((width, width), F32)),
        [sspec(), vspec(), vspec(), vspec(), vspec()],
        scratch=[pltpu.VMEM((width, width), BF16), pltpu.VMEM((rows_dev, width), BF16)],
    )(core_s, wt_own, wt_oth, agg_own, agg_oth)
    return hidden[None], weights[None]


def solution(mesh):
    n_tm = mesh.shape["tm"]
    fine = Mesh(mesh.devices.reshape(X, Y, C, n_tm), ("x", "y", "c", "z"))
    dom = ("x", "y", "c")
    in_specs = (
        P("z", dom, None),
        P("z", dom),
        P("z", dom),
        P("z", dom, None, None),
        P("z", dom),
        P(),
        P(),
        P(),
        P(),
        P(),
    )
    out_specs = (P("z", dom, None), P("z", None, None))
    return jax.shard_map(layer, mesh=fine, in_specs=in_specs, out_specs=out_specs, check_vma=False)
```

```python
import functools

import jax
import jax.numpy as jnp
from jax import lax
from jax.experimental import pallas as pl
from jax.experimental.pallas import tpu as pltpu
from jax.sharding import Mesh, PartitionSpec as P


BLOCK = 128
X, Y, C = 4, 4, 2
CHIPS = X * Y
F32 = jnp.float32
BF16 = jnp.bfloat16
VM = pltpu.MemorySpace.VMEM
SM = pltpu.MemorySpace.SMEM
HB = pltpu.MemorySpace.HBM
NN = (((1,), (0,)), ((), ()))
NT = (((1,), (1,)), ((), ()))
TN = (((0,), (0,)), ((), ()))


def mm(a, b, dims):
    return lax.dot_general(a, b, dims, preferred_element_type=F32)


def vspec():
    return pl.BlockSpec(memory_space=VM)


def hspec():
    return pl.BlockSpec(memory_space=HB)


def sspec():
    return pl.BlockSpec(memory_space=SM)


def call(kernel, out_shape, in_specs, scratch=(), flops=10**8, bytes_accessed=10**6, vmem_mib=8, out=None):
    many = isinstance(out_shape, (tuple, list))
    return pl.pallas_call(
        kernel,
        out_shape=out_shape,
        in_specs=in_specs,
        out_specs=out or (tuple(vspec() for _ in out_shape) if many else vspec()),
        scratch_shapes=list(scratch),
        cost_estimate=pl.CostEstimate(flops=flops, bytes_accessed=bytes_accessed, transcendentals=0),
        compiler_params=pltpu.CompilerParams(vmem_limit_bytes=vmem_mib * 2**20),
    )


def place():
    return tuple(lax.axis_index(axis).astype(jnp.int32) for axis in ("x", "y", "c", "z"))


def pool_kernel(feat_hbm, pool_hbm, send_ref, keep_ref, mine_ref, give_ref, feat_ref, pool_ref, sems):
    fetch = [pltpu.make_async_copy(feat_hbm, feat_ref, sems.at[0]), pltpu.make_async_copy(pool_hbm, pool_ref, sems.at[1])]
    for cp in fetch:
        cp.start()
    for cp in fetch:
        cp.wait()
    half = send_ref.shape[0]
    core = place()[2]
    own = pl.multiple_of(core * half, half)
    other = pl.multiple_of((1 - core) * half, half)
    feat = feat_ref[...]
    gates = jax.nn.sigmoid(mm(feat, pool_ref[:, pl.ds(other, half)], NN)).astype(BF16)
    send_ref[...] = mm(gates, feat, TN).astype(BF16)
    gates = jax.nn.sigmoid(mm(feat, pool_ref[:, pl.ds(own, half)], NN)).astype(BF16)
    keep_ref[...] = mm(gates, feat, TN)
    mine_ref[...] = feat_ref[:, pl.ds(own, half)]
    give_ref[...] = feat_ref[:, pl.ds(other, half)]


def join_kernel(*refs):
    pieces, (low, high, sems) = refs[:-3], refs[-3:]
    half = len(pieces) // 2
    copies = []
    for n, piece in enumerate(pieces):
        out = low if n < half else high
        size = piece.shape[0]
        cp = pltpu.make_async_copy(piece, out.at[pl.ds((n % half) * size, size)], sems.at[n])
        cp.start()
        copies.append(cp)
    for cp in copies:
        cp.wait()


def join(a, b):
    shape = jax.ShapeDtypeStruct((len(a) * a[0].shape[0],) + a[0].shape[1:], a[0].dtype)
    pieces = a + b
    return call(
        join_kernel,
        (shape, shape),
        [pl.BlockSpec(memory_space=pl.ANY)] * len(pieces),
        scratch=[pltpu.SemaphoreType.DMA((len(pieces),))],
        flops=0,
    )(*pieces)


def sum_kernel(scale, parts_ref, out_ref):
    total = jnp.sum(parts_ref[...].astype(F32), axis=0) * scale
    out_ref[...] = jnp.broadcast_to(total.astype(BF16)[None], out_ref.shape)


def chain_kernel(summ_ref, w_in_ref, w_ref, offset_ref, start_ref, out_ref, side_ref, startt_ref):
    n_t, cols, width = summ_ref.shape
    x, y, core, last = place()
    col0 = core * (width // C) + (x * Y + y) * cols
    window = pl.multiple_of((col0 // BLOCK) * BLOCK, BLOCK)
    startt_ref[...] = start_ref[:, pl.ds(window, BLOCK)].T
    summ = summ_ref[...].reshape(n_t * cols, width)
    for g in range(3):
        side = mm(summ, w_in_ref[g], NT)
        if g == 0:
            side = side - offset_ref[...]
        side_ref[g] = side.reshape(n_t, cols, width)
    state = startt_ref[pl.ds(pl.multiple_of(lax.rem(col0, BLOCK), cols), cols), :]

    def step(t, state):
        state_b = state.astype(BF16)
        update = jax.nn.sigmoid(side_ref[0, t] + mm(state_b, w_ref[0], NT))
        reset = jax.nn.sigmoid(side_ref[1, t] + mm(state_b, w_ref[1], NT))
        cand = jnp.tanh(side_ref[2, t] + mm((reset * state).astype(BF16), w_ref[2], NT))
        return (1.0 - update) * state + update * cand

    state = lax.fori_loop(0, last + 1, step, state)
    out_ref[...] = jnp.broadcast_to(state.astype(BF16)[None], out_ref.shape)


def masked(rows, used, tiles, lhs):
    for j in range(tiles.shape[0]):
        tile = tiles[j]
        at = jnp.where(j < used[0, 0], rows[0, j] & 1, 2)
        for r in range(2):
            lhs[r * BLOCK : (r + 1) * BLOCK, j * BLOCK : (j + 1) * BLOCK] = jnp.where(
                at == r, tile, jnp.zeros_like(tile)
            )


def slot_of(step):
    return jnp.where(step == 0, 0, jnp.where(step == 3, 1, step + 1))


def agg_oth_kernel(cols_own, cols_oth, rows_oth, used_oth, tiles, feat, *refs):
    pieces, (agg, rhs_own, blocks, rhs, lhs, sems) = refs[:-6], refs[-6:]
    copies = []
    first = 0
    for n, piece in enumerate(pieces):
        cp = pltpu.make_async_copy(piece, blocks.at[pl.ds(first, piece.shape[0])], sems.at[n])
        cp.start()
        copies.append(cp)
        first += piece.shape[0]
    masked(rows_oth, used_oth, tiles, lhs)
    for cp in copies:
        cp.wait()
    x, y, core, _ = place()
    for cols, out in ((cols_oth, rhs), (cols_own, rhs_own)):
        for j in range(tiles.shape[0]):
            col = cols[0, j]
            owner = col >> 1
            in_x = slot_of(((owner >> 3) - x) & 3)
            in_y = slot_of(((owner >> 1) - y) & 3)
            slot = jnp.where((owner & 1) == core, in_y * 4 + in_x, in_x * 4 + in_y + CHIPS)
            out[j * BLOCK : (j + 1) * BLOCK, :] = blocks[slot * 2 + (col & 1)]
    agg[...] = (feat[...].astype(F32) + mm(lhs[...], rhs[...], NN)).astype(BF16)


def agg_own_kernel(rows, used, tiles, feat, rhs, agg, lhs):
    masked(rows, used, tiles, lhs)
    agg[...] = (feat[...].astype(F32) + mm(lhs[...], rhs[...], NN)).astype(BF16)


def final_kernel(wt_own, wt_oth, agg_own, agg_oth, hid_ref, w_ref, wt, agg):
    half = wt_own.shape[0]
    core = place()[2]
    own = pl.multiple_of(core * half, half)
    oth = pl.multiple_of((1 - core) * half, half)
    wt[pl.ds(own, half), :] = wt_own[...]
    wt[pl.ds(oth, half), :] = wt_oth[...]
    agg[:, pl.ds(own, half)] = agg_own[...]
    agg[:, pl.ds(oth, half)] = agg_oth[...]
    width = wt.shape[0]
    mixed = mm(agg[...], wt[...], NT)
    hid_ref[...] = jnp.maximum(mixed * width ** (-0.5), 0.0).astype(BF16)
    w_ref[...] = wt[...].astype(F32).T


def swap(x):
    return lax.ppermute(x, "c", [(0, 1), (1, 0)])


def trade(x, axes):
    return lax.all_to_all(x, axes, split_axis=0, concat_axis=0, tiled=True)


def shift(x, axis, distance):
    size = lax.axis_size(axis)
    return lax.ppermute(x, axis, [(i, (i + distance) % size) for i in range(size)])


def spread(x, axis):
    return [x] + [shift(x, axis, step) for step in (1, -1, 2)]


def layer(
    features,
    tile_rows,
    tile_cols,
    tile_vals,
    tile_used,
    pool_weight,
    w_in,
    w_state,
    gate_offset,
    start_weight,
):
    rows_dev, width = features.shape[1:]
    slots = tile_rows.shape[1]
    half = width // 2
    n_tm = lax.axis_size("z")
    feat = features[0]
    blocks_dev = rows_dev // BLOCK

    bf_half = jax.ShapeDtypeStruct((half, width), BF16)
    feat_half = jax.ShapeDtypeStruct((rows_dev, half), BF16)
    send, keep, feat_mine, feat_give = call(
        pool_kernel,
        (bf_half, jax.ShapeDtypeStruct((half, width), F32), feat_half, feat_half),
        [hspec(), hspec()],
        scratch=[pltpu.VMEM(feat.shape, BF16), pltpu.VMEM(pool_weight.shape, BF16), pltpu.SemaphoreType.DMA((2,))],
    )(feat, pool_weight)
    partial = (keep + swap(send).astype(F32)).astype(BF16)
    cols = half // CHIPS
    parts = trade(partial.reshape(CHIPS, cols, width), ("x", "y"))
    snaps = jax.ShapeDtypeStruct((n_tm, cols, width), BF16)
    scale = (rows_dev * CHIPS * C) ** (-0.5)
    summ = call(functools.partial(sum_kernel, scale), snaps, [vspec()], flops=10**7)(parts)
    summ = trade(summ, "z")

    feat_oth = swap(feat_give)
    four = (blocks_dev, BLOCK, half)
    blocks_a = spread(feat_mine.reshape(four), "x")
    blocks_b = spread(feat_oth.reshape(four), "y")
    joined_a, joined_b = join(blocks_a, blocks_b)
    gathered = spread(joined_a, "y") + spread(joined_b, "x")

    rows_oth, cols_oth, used_oth = swap(tile_rows), swap(tile_cols), swap(tile_used)
    tiles_own = tile_vals[0]
    tiles_oth = swap(tiles_own)
    depth = slots * BLOCK
    lhs = pltpu.VMEM((rows_dev, depth), BF16)
    agg_give, rhs_own = call(
        agg_oth_kernel,
        (feat_half, jax.ShapeDtypeStruct((depth, half), BF16)),
        [sspec()] * 4 + [vspec()] * 2 + [pl.BlockSpec(memory_space=pl.ANY)] * len(gathered),
        scratch=[
            pltpu.VMEM((CHIPS * C * blocks_dev, BLOCK, half), BF16),
            pltpu.VMEM((depth, half), BF16),
            lhs,
            pltpu.SemaphoreType.DMA((len(gathered),)),
        ],
        vmem_mib=16,
    )(tile_cols, cols_oth, rows_oth, used_oth, tiles_oth, feat_oth, *gathered)
    agg_oth = swap(agg_give)
    agg_own = call(
        agg_own_kernel, feat_half, [sspec()] * 2 + [vspec()] * 3, scratch=[lhs], vmem_mib=8
    )(tile_rows, tile_used, tiles_own, feat_mine, rhs_own)

    evolved = call(
        chain_kernel,
        jax.ShapeDtypeStruct((CHIPS, cols, width), BF16),
        [vspec()] * 5,
        scratch=[
            pltpu.VMEM((3, n_tm, cols, width), F32),
            pltpu.VMEM((BLOCK, width), F32),
        ],
        vmem_mib=8,
    )(summ, w_in, w_state, gate_offset[None, :], start_weight)
    wt_own = trade(evolved, ("x", "y")).reshape(half, width)
    wt_oth = swap(wt_own)
    hidden, weights = call(
        final_kernel,
        (jax.ShapeDtypeStruct((rows_dev, width), BF16), jax.ShapeDtypeStruct((width, width), F32)),
        [vspec(), vspec(), vspec(), vspec()],
        scratch=[pltpu.VMEM((width, width), BF16), pltpu.VMEM((rows_dev, width), BF16)],
    )(wt_own, wt_oth, agg_own, agg_oth)
    return hidden[None], weights[None]


def solution(mesh):
    n_tm = mesh.shape["tm"]
    fine = Mesh(mesh.devices.reshape(X, Y, C, n_tm), ("x", "y", "c", "z"))
    dom = ("x", "y", "c")
    in_specs = (
        P("z", dom, None),
        P("z", dom),
        P("z", dom),
        P("z", dom, None, None),
        P("z", dom),
        P(),
        P(),
        P(),
        P(),
        P(),
    )
    out_specs = (P("z", dom, None), P("z", None, None))
    return jax.shard_map(layer, mesh=fine, in_specs=in_specs, out_specs=out_specs, check_vma=False)
```

```python
import functools

import jax
import jax.numpy as jnp
from jax import lax
from jax.experimental import pallas as pl
from jax.experimental.pallas import tpu as pltpu
from jax.sharding import Mesh, PartitionSpec as P


BLOCK = 128
X, Y, C = 4, 4, 2
PAIR = 2
CHIPS = X * Y
F32 = jnp.float32
BF16 = jnp.bfloat16
VM = pltpu.MemorySpace.VMEM
SM = pltpu.MemorySpace.SMEM
HB = pltpu.MemorySpace.HBM
NN = (((1,), (0,)), ((), ()))
NT = (((1,), (1,)), ((), ()))
TN = (((0,), (0,)), ((), ()))


def mm(a, b, dims):
    return lax.dot_general(a, b, dims, preferred_element_type=F32)


def vspec():
    return pl.BlockSpec(memory_space=VM)


def hspec():
    return pl.BlockSpec(memory_space=HB)


def sspec():
    return pl.BlockSpec(memory_space=SM)


def call(kernel, out_shape, in_specs, scratch=(), flops=10**8, bytes_accessed=10**6, vmem_mib=8, out=None):
    many = isinstance(out_shape, (tuple, list))
    return pl.pallas_call(
        kernel,
        out_shape=out_shape,
        in_specs=in_specs,
        out_specs=out or (tuple(vspec() for _ in out_shape) if many else vspec()),
        scratch_shapes=list(scratch),
        cost_estimate=pl.CostEstimate(flops=flops, bytes_accessed=bytes_accessed, transcendentals=0),
        compiler_params=pltpu.CompilerParams(vmem_limit_bytes=vmem_mib * 2**20),
    )


def place():
    return tuple(lax.axis_index(axis).astype(jnp.int32) for axis in ("x", "y", "c", "z"))


def pool_kernel(
    feat_hbm, pool_hbm, send_ref, keep_ref, mine_hbm, give_ref, feat_ref, pool_ref, mine_ref, sems
):
    fetch = [pltpu.make_async_copy(feat_hbm, feat_ref, sems.at[0]), pltpu.make_async_copy(pool_hbm, pool_ref, sems.at[1])]
    for cp in fetch:
        cp.start()
    for cp in fetch:
        cp.wait()
    half = send_ref.shape[0]
    core = place()[2]
    own = pl.multiple_of(core * half, half)
    other = pl.multiple_of((1 - core) * half, half)
    feat = feat_ref[...]
    gates = jax.nn.sigmoid(mm(feat, pool_ref[:, pl.ds(other, half)], NN)).astype(BF16)
    send_ref[...] = mm(gates, feat, TN).astype(BF16)
    gates = jax.nn.sigmoid(mm(feat, pool_ref[:, pl.ds(own, half)], NN)).astype(BF16)
    mine_ref[...] = feat_ref[:, pl.ds(own, half)]
    give_ref[...] = feat_ref[:, pl.ds(other, half)]
    store = pltpu.make_async_copy(mine_ref, mine_hbm, sems.at[2])
    store.start()
    keep_ref[...] = mm(gates, feat, TN)
    store.wait()


def column0(width):
    x, y, core, z = place()
    return core * (width // C) + ((x * Y + y) * lax.axis_size("z") + z) * PAIR


def pack_kernel(keep_ref, recv_ref, out_hbm, out_ref, sem, rows_ref, tiles_ref):
    n = rows_ref.shape[1] // PAIR
    for b in range(rows_ref.shape[0]):
        at = slice(b * BLOCK, (b + 1) * BLOCK)
        rows_ref[b] = keep_ref[:, at] + recv_ref[:, at].astype(F32)
        for i in range(PAIR):
            tiles_ref[pl.ds(PAIR * b + i, n, stride=8), :] = rows_ref[b, pl.ds(i, n, stride=PAIR), :]
    out_ref[...] = tiles_ref[...].astype(BF16)
    store = pltpu.make_async_copy(out_ref, out_hbm, sem)
    store.start()
    store.wait()


def unpack(packed_ref, tiles_ref, rows_ref):
    tiles_ref[...] = packed_ref[...].astype(F32)
    n = rows_ref.shape[1] // PAIR
    for b in range(rows_ref.shape[0]):
        for i in range(PAIR):
            rows_ref[b, pl.ds(i, n, stride=PAIR), :] = tiles_ref[pl.ds(PAIR * b + i, n, stride=8), :]


def join_kernel(*refs):
    pieces, (start_hbm, low, high, startt_hbm, start_ref, turned_ref, startt, sems) = refs[:-8], refs[-8:]
    half = len(pieces) // 2
    copies = []
    for n, piece in enumerate(pieces):
        out = low if n < half else high
        size = piece.shape[0]
        cp = pltpu.make_async_copy(piece, out.at[pl.ds((n % half) * size, size)], sems.at[n])
        cp.start()
        copies.append(cp)
    col0 = column0(start_hbm.shape[1])
    window = pl.multiple_of((col0 // BLOCK) * BLOCK, BLOCK)
    cp = pltpu.make_async_copy(start_hbm.at[:, pl.ds(window, BLOCK)], start_ref, sems.at[len(pieces)])
    cp.start()
    cp.wait()
    turned_ref[...] = start_ref[...].T
    row0 = lax.rem(col0, BLOCK)
    skip = lax.rem(row0, 8)
    rows = turned_ref[pl.ds(pl.multiple_of(row0 - skip, 8), 8), :]
    startt[...] = pltpu.roll(rows, lax.rem(8 - skip, 8), 0)
    store = pltpu.make_async_copy(startt, startt_hbm, sems.at[len(pieces) + 1])
    store.start()
    store.wait()
    for cp in copies:
        cp.wait()


def in_hbm(x):
    return pltpu.with_memory_space_constraint(x, HB)


def join(a, b, start_weight):
    shape = jax.ShapeDtypeStruct((len(a) * a[0].shape[0],) + a[0].shape[1:], a[0].dtype)
    pieces = a + b
    rows = start_weight.shape[0]
    return call(
        join_kernel,
        (shape, shape, pltpu.HBM((8, rows), F32)),
        [pl.BlockSpec(memory_space=pl.ANY)] * len(pieces) + [hspec()],
        out=(vspec(), vspec(), hspec()),
        scratch=[
            pltpu.VMEM((rows, BLOCK), F32),
            pltpu.VMEM((BLOCK, rows), F32),
            pltpu.VMEM((8, rows), F32),
            pltpu.SemaphoreType.DMA((len(pieces) + 2,)),
        ],
        flops=0,
    )(*pieces, in_hbm(start_weight))


def chain_kernel(
    scale, parts_ref, w_in_ref, w_ref, offset_ref, start_hbm, out_hbm, side_ref, hist_ref, start_ref, out_ref, sems
):
    fetch = pltpu.make_async_copy(start_hbm, start_ref, sems.at[0])
    fetch.start()
    _, n_t, sub, lanes = parts_ref.shape
    width = w_ref.shape[2]
    lane_blocks = width // lanes
    total = (jnp.sum(parts_ref[...].astype(F32), axis=0) * scale).reshape(n_t * sub, lanes)
    pieces = [total] + [pltpu.roll(total, n_t * sub - PAIR * b, 0) for b in range(1, lane_blocks)]
    summ = jnp.concatenate(pieces, axis=1).astype(BF16)
    for g in range(3):
        side = mm(summ, w_in_ref[g], NT)
        if g == 0:
            side = side - offset_ref[...]
        side_ref[g] = side.reshape(n_t, sub, width)
    fetch.wait()
    state = start_ref[...]
    row_pair = lax.broadcasted_iota(jnp.int32, (sub, lanes), 0) // PAIR

    def step(t, state):
        state_b = state.astype(BF16)
        update = jax.nn.sigmoid(side_ref[0, t] + mm(state_b, w_ref[0], NT))
        reset = jax.nn.sigmoid(side_ref[1, t] + mm(state_b, w_ref[1], NT))
        cand = jnp.tanh(side_ref[2, t] + mm((reset * state).astype(BF16), w_ref[2], NT))
        state = (1.0 - update) * state + update * cand
        tile = state[:, :lanes]
        for b in range(1, lane_blocks):
            tile = jnp.where(row_pair == b, pltpu.roll(state[:, b * lanes : (b + 1) * lanes], PAIR * b, 0), tile)
        hist_ref[t] = tile
        return state

    lax.fori_loop(0, n_t, step, state)
    out_ref[...] = jnp.broadcast_to(hist_ref[...].astype(BF16)[None], out_ref.shape)
    store = pltpu.make_async_copy(out_ref, out_hbm, sems.at[1])
    store.start()
    store.wait()


def masked(rows, used, tiles, lhs):
    for j in range(tiles.shape[0]):
        tile = tiles[j]
        at = jnp.where(j < used[0, 0], rows[0, j] & 1, 2)
        for r in range(2):
            lhs[r * BLOCK : (r + 1) * BLOCK, j * BLOCK : (j + 1) * BLOCK] = jnp.where(
                at == r, tile, jnp.zeros_like(tile)
            )


def slot_of(step):
    return jnp.where(step == 0, 0, jnp.where(step == 3, 1, step + 1))


def mask_kernel(rows_oth, used_oth, tiles_oth, rows_own, used_own, tiles_hbm, lhs_oth, lhs_own, tiles_own, sem):
    fetch = pltpu.make_async_copy(tiles_hbm, tiles_own, sem)
    fetch.start()
    masked(rows_oth, used_oth, tiles_oth, lhs_oth)
    fetch.wait()
    masked(rows_own, used_own, tiles_own, lhs_own)


def agg_oth_kernel(cols_own, cols_oth, lhs, feat, *refs):
    pieces, (agg, rhs_own, blocks, rhs, sems) = refs[:-5], refs[-5:]
    copies = []
    first = 0
    for n, piece in enumerate(pieces):
        cp = pltpu.make_async_copy(piece, blocks.at[pl.ds(first, piece.shape[0])], sems.at[n])
        cp.start()
        copies.append(cp)
        first += piece.shape[0]
    for cp in copies:
        cp.wait()
    x, y, core, _ = place()
    for cols, out in ((cols_oth, rhs), (cols_own, rhs_own)):
        for j in range(cols.shape[1]):
            col = cols[0, j]
            owner = col >> 1
            in_x = slot_of(((owner >> 3) - x) & 3)
            in_y = slot_of(((owner >> 1) - y) & 3)
            slot = jnp.where((owner & 1) == core, in_y * 4 + in_x, in_x * 4 + in_y + CHIPS)
            out[j * BLOCK : (j + 1) * BLOCK, :] = blocks[slot * 2 + (col & 1)]
    agg[...] = (feat[...].astype(F32) + mm(lhs[...], rhs[...], NN)).astype(BF16)


def agg_own_kernel(lhs, feat, rhs, agg):
    agg[...] = (feat[...].astype(F32) + mm(lhs[...], rhs[...], NN)).astype(BF16)


def final_kernel(wt_own, wt_oth, agg_own, agg_oth, hid_ref, w_ref, tiles, wt_f32, wt, agg):
    half = wt_f32.shape[1]
    core = place()[2]
    own = pl.multiple_of(core * half, half)
    oth = pl.multiple_of((1 - core) * half, half)
    for packed, at in ((wt_own, own), (wt_oth, oth)):
        unpack(packed, tiles, wt_f32)
        for b in range(wt_f32.shape[0]):
            lanes = slice(b * BLOCK, (b + 1) * BLOCK)
            wt[pl.ds(at, half), lanes] = wt_f32[b].astype(BF16)
            w_ref[lanes, pl.ds(at, half)] = wt_f32[b].T
    agg[:, pl.ds(own, half)] = agg_own[...]
    agg[:, pl.ds(oth, half)] = agg_oth[...]
    width = wt.shape[0]
    mixed = mm(agg[...], wt[...], NT)
    hid_ref[...] = jnp.maximum(mixed * width ** (-0.5), 0.0).astype(BF16)


def swap(x):
    return lax.ppermute(x, "c", [(0, 1), (1, 0)])


def trade(x, axes):
    return lax.all_to_all(x, axes, split_axis=0, concat_axis=0, tiled=True)


def shift(x, axis, distance):
    size = lax.axis_size(axis)
    return lax.ppermute(x, axis, [(i, (i + distance) % size) for i in range(size)])


def spread(x, axis):
    return [x] + [shift(x, axis, step) for step in (1, -1, 2)]


def layer(
    features,
    tile_rows,
    tile_cols,
    tile_vals,
    tile_used,
    pool_weight,
    w_in,
    w_state,
    gate_offset,
    start_weight,
):
    rows_dev, width = features.shape[1:]
    slots = tile_rows.shape[1]
    half = width // 2
    n_tm = lax.axis_size("z")
    feat = features[0]
    blocks_dev = rows_dev // BLOCK

    bf_half = jax.ShapeDtypeStruct((half, width), BF16)
    feat_half = jax.ShapeDtypeStruct((rows_dev, half), BF16)
    send, keep, feat_mine, feat_give = call(
        pool_kernel,
        (bf_half, jax.ShapeDtypeStruct((half, width), F32), pltpu.HBM(feat_half.shape, BF16), feat_half),
        [hspec(), hspec()],
        out=(vspec(), vspec(), hspec(), vspec()),
        scratch=[
            pltpu.VMEM(feat.shape, BF16),
            pltpu.VMEM(pool_weight.shape, BF16),
            pltpu.VMEM(feat_half.shape, BF16),
            pltpu.SemaphoreType.DMA((3,)),
        ],
    )(in_hbm(feat), in_hbm(pool_weight))
    packed = jax.ShapeDtypeStruct((half // PAIR * 8, BLOCK), BF16)
    partial = call(
        pack_kernel,
        pltpu.HBM(packed.shape, BF16),
        [vspec(), vspec()],
        out=hspec(),
        scratch=[pltpu.VMEM(packed.shape, BF16), pltpu.SemaphoreType.DMA(()), pltpu.VMEM((width // BLOCK, half, BLOCK), F32), pltpu.VMEM(packed.shape, F32)],
    )(keep, swap(send))
    everyone = ("x", "y", "z")
    parts = trade(partial.reshape(CHIPS * n_tm, 8, BLOCK), everyone)

    feat_oth = swap(feat_give)
    four = (blocks_dev, BLOCK, half)
    blocks_a = spread(feat_mine.reshape(four), "x")
    blocks_b = spread(feat_oth.reshape(four), "y")
    joined_a, joined_b, startt = join(blocks_a, blocks_b, start_weight)
    gathered = spread(joined_a, "y") + spread(joined_b, "x")

    rows_oth, cols_oth, used_oth = swap(tile_rows), swap(tile_cols), swap(tile_used)
    tiles_own = tile_vals[0]
    tiles_oth = swap(tiles_own)
    depth = slots * BLOCK
    lhs = jax.ShapeDtypeStruct((rows_dev, depth), BF16)
    lhs_oth, lhs_own = call(
        mask_kernel,
        (lhs, lhs),
        [sspec(), sspec(), vspec(), sspec(), sspec(), hspec()],
        scratch=[pltpu.VMEM(tiles_own.shape, BF16), pltpu.SemaphoreType.DMA(())],
    )(rows_oth, used_oth, tiles_oth, tile_rows, tile_used, in_hbm(tiles_own))
    agg_give, rhs_own = call(
        agg_oth_kernel,
        (feat_half, jax.ShapeDtypeStruct((depth, half), BF16)),
        [sspec()] * 2 + [vspec()] * 2 + [pl.BlockSpec(memory_space=pl.ANY)] * len(gathered),
        scratch=[
            pltpu.VMEM((CHIPS * C * blocks_dev, BLOCK, half), BF16),
            pltpu.VMEM((depth, half), BF16),
            pltpu.SemaphoreType.DMA((len(gathered),)),
        ],
        vmem_mib=16,
    )(tile_cols, cols_oth, lhs_oth, feat_oth, *gathered)
    agg_oth = swap(agg_give)
    agg_own = call(agg_own_kernel, feat_half, [vspec()] * 3)(lhs_own, feat_mine, rhs_own)

    scale = (rows_dev * CHIPS * C) ** (-0.5)
    evolved = call(
        functools.partial(chain_kernel, scale),
        pltpu.HBM((CHIPS, n_tm, 8, BLOCK), BF16),
        [vspec()] * 4 + [hspec()],
        out=hspec(),
        scratch=[
            pltpu.VMEM((3, n_tm, 8, width), F32),
            pltpu.VMEM((n_tm, 8, BLOCK), F32),
            pltpu.VMEM((8, width), F32),
            pltpu.VMEM((CHIPS, n_tm, 8, BLOCK), BF16),
            pltpu.SemaphoreType.DMA((2,)),
        ],
    )(parts.reshape(CHIPS, n_tm, 8, BLOCK), w_in, w_state, gate_offset[None, :], startt)
    wt_own = trade(evolved.reshape(CHIPS * n_tm, 8, BLOCK), everyone).reshape(packed.shape)
    wt_oth = swap(wt_own)
    hidden, weights = call(
        final_kernel,
        (jax.ShapeDtypeStruct((rows_dev, width), BF16), jax.ShapeDtypeStruct((width, width), F32)),
        [vspec()] * 4,
        scratch=[
            pltpu.VMEM(packed.shape, F32),
            pltpu.VMEM((width // BLOCK, half, BLOCK), F32),
            pltpu.VMEM((width, width), BF16),
            pltpu.VMEM((rows_dev, width), BF16),
        ],
    )(wt_own, wt_oth, agg_own, agg_oth)
    return hidden[None], weights[None]


def solution(mesh):
    n_tm = mesh.shape["tm"]
    fine = Mesh(mesh.devices.reshape(X, Y, C, n_tm), ("x", "y", "c", "z"))
    dom = ("x", "y", "c")
    in_specs = (
        P("z", dom, None),
        P("z", dom),
        P("z", dom),
        P("z", dom, None, None),
        P("z", dom),
        P(),
        P(),
        P(),
        P(),
        P(),
    )
    out_specs = (P("z", dom, None), P("z", None, None))
    return jax.shard_map(layer, mesh=fine, in_specs=in_specs, out_specs=out_specs, check_vma=False)
```

```python
import functools

import jax
import jax.numpy as jnp
from jax import lax
from jax.experimental import pallas as pl
from jax.experimental.pallas import tpu as pltpu
from jax.sharding import Mesh, PartitionSpec as P


BLOCK = 128
X, Y, C = 4, 4, 2
CHIPS = X * Y
F32 = jnp.float32
BF16 = jnp.bfloat16
VM = pltpu.MemorySpace.VMEM
SM = pltpu.MemorySpace.SMEM
HB = pltpu.MemorySpace.HBM
NN = (((1,), (0,)), ((), ()))
NT = (((1,), (1,)), ((), ()))
TN = (((0,), (0,)), ((), ()))


def mm(a, b, dims):
    return lax.dot_general(a, b, dims, preferred_element_type=F32)


def vspec():
    return pl.BlockSpec(memory_space=VM)


def hspec():
    return pl.BlockSpec(memory_space=HB)


def sspec():
    return pl.BlockSpec(memory_space=SM)


def call(kernel, out_shape, in_specs, scratch=(), flops=10**8, bytes_accessed=10**6, vmem_mib=8, out=None):
    many = isinstance(out_shape, (tuple, list))
    return pl.pallas_call(
        kernel,
        out_shape=out_shape,
        in_specs=in_specs,
        out_specs=out or (tuple(vspec() for _ in out_shape) if many else vspec()),
        scratch_shapes=list(scratch),
        cost_estimate=pl.CostEstimate(flops=flops, bytes_accessed=bytes_accessed, transcendentals=0),
        compiler_params=pltpu.CompilerParams(vmem_limit_bytes=vmem_mib * 2**20),
    )


def place():
    return tuple(lax.axis_index(axis).astype(jnp.int32) for axis in ("x", "y", "c", "z"))


def pool_kernel(
    feat_hbm, pool_hbm, send_ref, keep_ref, mine_hbm, give_ref, feat_ref, pool_ref, mine_ref, sems
):
    fetch = [pltpu.make_async_copy(feat_hbm, feat_ref, sems.at[0]), pltpu.make_async_copy(pool_hbm, pool_ref, sems.at[1])]
    for cp in fetch:
        cp.start()
    for cp in fetch:
        cp.wait()
    half = send_ref.shape[0]
    core = place()[2]
    own = pl.multiple_of(core * half, half)
    other = pl.multiple_of((1 - core) * half, half)
    feat = feat_ref[...]
    gates = jax.nn.sigmoid(mm(feat, pool_ref[:, pl.ds(other, half)], NN)).astype(BF16)
    send_ref[...] = mm(gates, feat, TN).astype(BF16)
    gates = jax.nn.sigmoid(mm(feat, pool_ref[:, pl.ds(own, half)], NN)).astype(BF16)
    mine_ref[...] = feat_ref[:, pl.ds(own, half)]
    give_ref[...] = feat_ref[:, pl.ds(other, half)]
    store = pltpu.make_async_copy(mine_ref, mine_hbm, sems.at[2])
    store.start()
    keep_ref[...] = mm(gates, feat, TN)
    store.wait()


def in_hbm(x):
    return pltpu.with_memory_space_constraint(x, HB)


def join_kernel(*refs):
    pieces, (low, high, sems) = refs[:-3], refs[-3:]
    half = len(pieces) // 2
    copies = []
    for n, piece in enumerate(pieces):
        out = low if n < half else high
        size = piece.shape[0]
        cp = pltpu.make_async_copy(piece, out.at[pl.ds((n % half) * size, size)], sems.at[n])
        cp.start()
        copies.append(cp)
    for cp in copies:
        cp.wait()


def join(a, b):
    shape = jax.ShapeDtypeStruct((len(a) * a[0].shape[0],) + a[0].shape[1:], a[0].dtype)
    pieces = a + b
    return call(
        join_kernel,
        (shape, shape),
        [pl.BlockSpec(memory_space=pl.ANY)] * len(pieces),
        scratch=[pltpu.SemaphoreType.DMA((len(pieces),))],
        flops=0,
    )(*pieces)


def sum_kernel(scale, parts_ref, out_ref):
    total = jnp.sum(parts_ref[...].astype(F32), axis=0) * scale
    out_ref[...] = jnp.broadcast_to(total.astype(BF16)[None], out_ref.shape)


def chain_kernel(summ_ref, w_in_ref, w_ref, offset_ref, start_hbm, out_ref, side_ref, startt_ref, start_ref, sem):
    n_t, cols, width = summ_ref.shape
    x, y, core, last = place()
    col0 = core * (width // C) + (x * Y + y) * cols
    window = pl.multiple_of((col0 // BLOCK) * BLOCK, BLOCK)
    fetch = pltpu.make_async_copy(start_hbm.at[:, pl.ds(window, BLOCK)], start_ref, sem)
    fetch.start()
    summ = summ_ref[...].reshape(n_t * cols, width)
    for g in range(3):
        side = mm(summ, w_in_ref[g], NT)
        if g == 0:
            side = side - offset_ref[...]
        side_ref[g] = side.reshape(n_t, cols, width)
    fetch.wait()
    startt_ref[...] = start_ref[...].T
    state = startt_ref[pl.ds(pl.multiple_of(lax.rem(col0, BLOCK), cols), cols), :]

    def step(t, state):
        state_b = state.astype(BF16)
        update = jax.nn.sigmoid(side_ref[0, t] + mm(state_b, w_ref[0], NT))
        reset = jax.nn.sigmoid(side_ref[1, t] + mm(state_b, w_ref[1], NT))
        cand = jnp.tanh(side_ref[2, t] + mm((reset * state).astype(BF16), w_ref[2], NT))
        return (1.0 - update) * state + update * cand

    state = lax.fori_loop(0, last + 1, step, state)
    out_ref[...] = jnp.broadcast_to(state.astype(BF16)[None], out_ref.shape)


def masked(rows, used, tiles, lhs):
    for j in range(tiles.shape[0]):
        tile = tiles[j]
        at = jnp.where(j < used[0, 0], rows[0, j] & 1, 2)
        for r in range(2):
            lhs[r * BLOCK : (r + 1) * BLOCK, j * BLOCK : (j + 1) * BLOCK] = jnp.where(
                at == r, tile, jnp.zeros_like(tile)
            )


def slot_of(step):
    return jnp.where(step == 0, 0, jnp.where(step == 3, 1, step + 1))


def agg_oth_kernel(cols_own, cols_oth, rows_oth, used_oth, tiles, feat, *refs):
    pieces, (agg, rhs_own, blocks, rhs, lhs, sems) = refs[:-6], refs[-6:]
    copies = []
    first = 0
    for n, piece in enumerate(pieces):
        cp = pltpu.make_async_copy(piece, blocks.at[pl.ds(first, piece.shape[0])], sems.at[n])
        cp.start()
        copies.append(cp)
        first += piece.shape[0]
    masked(rows_oth, used_oth, tiles, lhs)
    for cp in copies:
        cp.wait()
    x, y, core, _ = place()
    for cols, out in ((cols_oth, rhs), (cols_own, rhs_own)):
        for j in range(tiles.shape[0]):
            col = cols[0, j]
            owner = col >> 1
            in_x = slot_of(((owner >> 3) - x) & 3)
            in_y = slot_of(((owner >> 1) - y) & 3)
            slot = jnp.where((owner & 1) == core, in_y * 4 + in_x, in_x * 4 + in_y + CHIPS)
            out[j * BLOCK : (j + 1) * BLOCK, :] = blocks[slot * 2 + (col & 1)]
    agg[...] = (feat[...].astype(F32) + mm(lhs[...], rhs[...], NN)).astype(BF16)


def agg_own_kernel(rows, used, tiles, feat, rhs, agg, lhs):
    masked(rows, used, tiles, lhs)
    agg[...] = (feat[...].astype(F32) + mm(lhs[...], rhs[...], NN)).astype(BF16)


def final_kernel(wt_own, wt_oth, agg_own, agg_oth, hid_ref, w_ref, wt, agg):
    half = wt_own.shape[0]
    core = place()[2]
    own = pl.multiple_of(core * half, half)
    oth = pl.multiple_of((1 - core) * half, half)
    wt[pl.ds(own, half), :] = wt_own[...]
    wt[pl.ds(oth, half), :] = wt_oth[...]
    agg[:, pl.ds(own, half)] = agg_own[...]
    agg[:, pl.ds(oth, half)] = agg_oth[...]
    width = wt.shape[0]
    mixed = mm(agg[...], wt[...], NT)
    hid_ref[...] = jnp.maximum(mixed * width ** (-0.5), 0.0).astype(BF16)
    w_ref[...] = wt[...].astype(F32).T


def swap(x):
    return lax.ppermute(x, "c", [(0, 1), (1, 0)])


def trade(x, axes):
    return lax.all_to_all(x, axes, split_axis=0, concat_axis=0, tiled=True)


def shift(x, axis, distance):
    size = lax.axis_size(axis)
    return lax.ppermute(x, axis, [(i, (i + distance) % size) for i in range(size)])


def spread(x, axis):
    return [x] + [shift(x, axis, step) for step in (1, -1, 2)]


def layer(
    features,
    tile_rows,
    tile_cols,
    tile_vals,
    tile_used,
    pool_weight,
    w_in,
    w_state,
    gate_offset,
    start_weight,
):
    rows_dev, width = features.shape[1:]
    slots = tile_rows.shape[1]
    half = width // 2
    n_tm = lax.axis_size("z")
    feat = features[0]
    blocks_dev = rows_dev // BLOCK

    bf_half = jax.ShapeDtypeStruct((half, width), BF16)
    feat_half = jax.ShapeDtypeStruct((rows_dev, half), BF16)
    send, keep, feat_mine, feat_give = call(
        pool_kernel,
        (bf_half, jax.ShapeDtypeStruct((half, width), F32), pltpu.HBM(feat_half.shape, BF16), feat_half),
        [hspec(), hspec()],
        out=(vspec(), vspec(), hspec(), vspec()),
        scratch=[
            pltpu.VMEM(feat.shape, BF16),
            pltpu.VMEM(pool_weight.shape, BF16),
            pltpu.VMEM(feat_half.shape, BF16),
            pltpu.SemaphoreType.DMA((3,)),
        ],
    )(in_hbm(feat), in_hbm(pool_weight))
    partial = (keep + swap(send).astype(F32)).astype(BF16)
    cols = half // CHIPS
    parts = trade(partial.reshape(CHIPS, cols, width), ("x", "y"))
    snaps = jax.ShapeDtypeStruct((n_tm, cols, width), BF16)
    scale = (rows_dev * CHIPS * C) ** (-0.5)
    summ = call(functools.partial(sum_kernel, scale), snaps, [vspec()], flops=10**7)(parts)
    summ = trade(summ, "z")

    feat_oth = swap(feat_give)
    four = (blocks_dev, BLOCK, half)
    blocks_a = spread(feat_mine.reshape(four), "x")
    blocks_b = spread(feat_oth.reshape(four), "y")
    joined_a, joined_b = join(blocks_a, blocks_b)
    gathered = spread(joined_a, "y") + spread(joined_b, "x")

    rows_oth, cols_oth, used_oth = swap(tile_rows), swap(tile_cols), swap(tile_used)
    tiles_own = tile_vals[0]
    tiles_oth = swap(tiles_own)
    depth = slots * BLOCK
    lhs = pltpu.VMEM((rows_dev, depth), BF16)
    agg_give, rhs_own = call(
        agg_oth_kernel,
        (feat_half, jax.ShapeDtypeStruct((depth, half), BF16)),
        [sspec()] * 4 + [vspec()] * 2 + [pl.BlockSpec(memory_space=pl.ANY)] * len(gathered),
        scratch=[
            pltpu.VMEM((CHIPS * C * blocks_dev, BLOCK, half), BF16),
            pltpu.VMEM((depth, half), BF16),
            lhs,
            pltpu.SemaphoreType.DMA((len(gathered),)),
        ],
        vmem_mib=16,
    )(tile_cols, cols_oth, rows_oth, used_oth, tiles_oth, feat_oth, *gathered)
    agg_oth = swap(agg_give)
    agg_own = call(
        agg_own_kernel, feat_half, [sspec()] * 2 + [vspec()] * 3, scratch=[lhs], vmem_mib=8
    )(tile_rows, tile_used, tiles_own, feat_mine, rhs_own)

    evolved = call(
        chain_kernel,
        jax.ShapeDtypeStruct((CHIPS, cols, width), BF16),
        [vspec()] * 4 + [hspec()],
        scratch=[
            pltpu.VMEM((3, n_tm, cols, width), F32),
            pltpu.VMEM((BLOCK, width), F32),
            pltpu.VMEM((width, BLOCK), F32),
            pltpu.SemaphoreType.DMA(()),
        ],
        vmem_mib=8,
    )(summ, w_in, w_state, gate_offset[None, :], in_hbm(start_weight))
    wt_own = trade(evolved, ("x", "y")).reshape(half, width)
    wt_oth = swap(wt_own)
    hidden, weights = call(
        final_kernel,
        (jax.ShapeDtypeStruct((rows_dev, width), BF16), jax.ShapeDtypeStruct((width, width), F32)),
        [vspec(), vspec(), vspec(), vspec()],
        scratch=[pltpu.VMEM((width, width), BF16), pltpu.VMEM((rows_dev, width), BF16)],
    )(wt_own, wt_oth, agg_own, agg_oth)
    return hidden[None], weights[None]


def solution(mesh):
    n_tm = mesh.shape["tm"]
    fine = Mesh(mesh.devices.reshape(X, Y, C, n_tm), ("x", "y", "c", "z"))
    dom = ("x", "y", "c")
    in_specs = (
        P("z", dom, None),
        P("z", dom),
        P("z", dom),
        P("z", dom, None, None),
        P("z", dom),
        P(),
        P(),
        P(),
        P(),
        P(),
    )
    out_specs = (P("z", dom, None), P("z", None, None))
    return jax.shard_map(layer, mesh=fine, in_specs=in_specs, out_specs=out_specs, check_vma=False)
```

```python
import functools

import jax
import jax.numpy as jnp
from jax import lax
from jax.experimental import pallas as pl
from jax.experimental.pallas import tpu as pltpu
from jax.sharding import Mesh, PartitionSpec as P


BLOCK = 128
X, Y, C = 4, 4, 2
CHIPS = X * Y
F32 = jnp.float32
BF16 = jnp.bfloat16
VM = pltpu.MemorySpace.VMEM
SM = pltpu.MemorySpace.SMEM
HB = pltpu.MemorySpace.HBM
NN = (((1,), (0,)), ((), ()))
NT = (((1,), (1,)), ((), ()))
TN = (((0,), (0,)), ((), ()))


def mm(a, b, dims):
    return lax.dot_general(a, b, dims, preferred_element_type=F32)


def vspec():
    return pl.BlockSpec(memory_space=VM)


def hspec():
    return pl.BlockSpec(memory_space=HB)


def sspec():
    return pl.BlockSpec(memory_space=SM)


def call(kernel, out_shape, in_specs, scratch=(), flops=10**8, bytes_accessed=10**6, vmem_mib=8, out=None):
    many = isinstance(out_shape, (tuple, list))
    return pl.pallas_call(
        kernel,
        out_shape=out_shape,
        in_specs=in_specs,
        out_specs=out or (tuple(vspec() for _ in out_shape) if many else vspec()),
        scratch_shapes=list(scratch),
        cost_estimate=pl.CostEstimate(flops=flops, bytes_accessed=bytes_accessed, transcendentals=0),
        compiler_params=pltpu.CompilerParams(vmem_limit_bytes=vmem_mib * 2**20),
    )


def place():
    return tuple(lax.axis_index(axis).astype(jnp.int32) for axis in ("x", "y", "c", "z"))


def pool_kernel(
    feat_hbm, pool_hbm, send_ref, keep_ref, mine_hbm, give_ref, feat_ref, pool_ref, mine_ref, sems
):
    fetch = [pltpu.make_async_copy(feat_hbm, feat_ref, sems.at[0]), pltpu.make_async_copy(pool_hbm, pool_ref, sems.at[1])]
    for cp in fetch:
        cp.start()
    for cp in fetch:
        cp.wait()
    half = send_ref.shape[0]
    core = place()[2]
    own = pl.multiple_of(core * half, half)
    other = pl.multiple_of((1 - core) * half, half)
    feat = feat_ref[...]
    gates = jax.nn.sigmoid(mm(feat, pool_ref[:, pl.ds(other, half)], NN)).astype(BF16)
    send_ref[...] = mm(gates, feat, TN).astype(BF16)
    gates = jax.nn.sigmoid(mm(feat, pool_ref[:, pl.ds(own, half)], NN)).astype(BF16)
    mine_ref[...] = feat_ref[:, pl.ds(own, half)]
    give_ref[...] = feat_ref[:, pl.ds(other, half)]
    store = pltpu.make_async_copy(mine_ref, mine_hbm, sems.at[2])
    store.start()
    keep_ref[...] = mm(gates, feat, TN)
    store.wait()


def in_hbm(x):
    return pltpu.with_memory_space_constraint(x, HB)


def join_kernel(*refs):
    pieces, (low, high, sems) = refs[:-3], refs[-3:]
    half = len(pieces) // 2
    copies = []
    for n, piece in enumerate(pieces):
        out = low if n < half else high
        size = piece.shape[0]
        cp = pltpu.make_async_copy(piece, out.at[pl.ds((n % half) * size, size)], sems.at[n])
        cp.start()
        copies.append(cp)
    for cp in copies:
        cp.wait()


def join(a, b):
    shape = jax.ShapeDtypeStruct((len(a) * a[0].shape[0],) + a[0].shape[1:], a[0].dtype)
    pieces = a + b
    return call(
        join_kernel,
        (shape, shape),
        [pl.BlockSpec(memory_space=pl.ANY)] * len(pieces),
        scratch=[pltpu.SemaphoreType.DMA((len(pieces),))],
        flops=0,
    )(*pieces)


def sum_kernel(scale, parts_ref, out_ref):
    total = jnp.sum(parts_ref[...].astype(F32), axis=0) * scale
    out_ref[...] = jnp.broadcast_to(total.astype(BF16)[None], out_ref.shape)


def prepare_kernel(
    tile_rows, tile_cols, used, w_in_hbm, w_state_hbm, start_hbm, w_in_t, w_state_t, start_t_hbm, slots, w_in, w_state, start_ref, turned_ref, start_t, sems
):
    cols, width = start_t.shape
    x, y, core, _ = place()
    col0 = core * (width // C) + (x * Y + y) * cols
    window = pl.multiple_of((col0 // BLOCK) * BLOCK, BLOCK)
    fetch = pltpu.make_async_copy(start_hbm.at[:, pl.ds(window, BLOCK)], start_ref, sems.at[0])
    fetch.start()
    copies = []
    for n, (src, dst) in enumerate(((w_in_hbm, w_in), (w_state_hbm, w_state))):
        for g in range(3):
            cp = pltpu.make_async_copy(src.at[g], dst.at[g], sems.at[2 + 3 * n + g])
            cp.start()
            copies.append(cp)
    for j in range(slots.shape[1]):
        slots[0, j] = tile_cols[0, j]
        slots[1, j] = jnp.where(j < used[0, 0], tile_rows[0, j] & 1, 2)
    fetch.wait()
    turned_ref[...] = start_ref[...].T
    start_t[...] = turned_ref[pl.ds(pl.multiple_of(lax.rem(col0, BLOCK), cols), cols), :]
    store = pltpu.make_async_copy(start_t, start_t_hbm, sems.at[1])
    store.start()
    for g in range(3):
        copies[g].wait()
        w_in_t[g] = w_in[g].T
    for g in range(3):
        copies[3 + g].wait()
        w_state_t[g] = w_state[g].T
    store.wait()


def chain_kernel(summ_ref, w_in_ref, w_ref, offset_ref, start_hbm, out_ref, side_ref, start_ref, sem):
    n_t, cols, width = summ_ref.shape
    fetch = pltpu.make_async_copy(start_hbm, start_ref, sem)
    fetch.start()
    summ = summ_ref[...].reshape(n_t * cols, width)
    for g in range(3):
        side = mm(summ, w_in_ref[g], NN)
        if g == 0:
            side = side - offset_ref[...]
        side_ref[g] = side.reshape(n_t, cols, width)

    def step(t, state):
        state_b = state.astype(BF16)
        reset = jax.nn.sigmoid(side_ref[1, t] + mm(state_b, w_ref[1], NN))
        update = jax.nn.sigmoid(side_ref[0, t] + mm(state_b, w_ref[0], NN))
        cand = jnp.tanh(side_ref[2, t] + mm((reset * state).astype(BF16), w_ref[2], NN))
        return (1.0 - update) * state + update * cand

    fetch.wait()
    state = lax.fori_loop(0, place()[3] + 1, step, start_ref[...])
    out_ref[...] = jnp.broadcast_to(state.astype(BF16)[None], out_ref.shape)


def masked(idx, tiles, lhs):
    for j in range(tiles.shape[0]):
        tile = tiles[j]
        for r in range(2):
            lhs[r * BLOCK : (r + 1) * BLOCK, j * BLOCK : (j + 1) * BLOCK] = jnp.where(
                idx[1, j] == r, tile, jnp.zeros_like(tile)
            )


def slot_of(step):
    return jnp.where(step == 0, 0, jnp.where(step == 3, 1, step + 1))


def agg_oth_kernel(idx_own, idx_oth, tiles, feat, *refs):
    pieces, (agg, rhs_own, blocks, rhs, lhs, sems) = refs[:-6], refs[-6:]
    copies = []
    first = 0
    for n, piece in enumerate(pieces):
        cp = pltpu.make_async_copy(piece, blocks.at[pl.ds(first, piece.shape[0])], sems.at[n])
        cp.start()
        copies.append(cp)
        first += piece.shape[0]
    masked(idx_oth, tiles, lhs)
    for cp in copies:
        cp.wait()
    x, y, core, _ = place()
    for idx, out in ((idx_oth, rhs), (idx_own, rhs_own)):
        for j in range(tiles.shape[0]):
            col = idx[0, j]
            owner = col >> 1
            in_x = slot_of(((owner >> 3) - x) & 3)
            in_y = slot_of(((owner >> 1) - y) & 3)
            slot = jnp.where((owner & 1) == core, in_y * 4 + in_x, in_x * 4 + in_y + CHIPS)
            out[j * BLOCK : (j + 1) * BLOCK, :] = blocks[slot * 2 + (col & 1)]
    agg[...] = (feat[...].astype(F32) + mm(lhs[...], rhs[...], NN)).astype(BF16)


def agg_own_kernel(idx, tiles, feat, rhs, agg, lhs):
    masked(idx, tiles, lhs)
    agg[...] = (feat[...].astype(F32) + mm(lhs[...], rhs[...], NN)).astype(BF16)


def final_kernel(wt_own, wt_oth, agg_own, agg_oth, hid_ref, w_ref, wt, agg):
    half = wt_own.shape[0]
    core = place()[2]
    own = pl.multiple_of(core * half, half)
    oth = pl.multiple_of((1 - core) * half, half)
    wt[pl.ds(own, half), :] = wt_own[...]
    wt[pl.ds(oth, half), :] = wt_oth[...]
    agg[:, pl.ds(own, half)] = agg_own[...]
    agg[:, pl.ds(oth, half)] = agg_oth[...]
    width = wt.shape[0]
    mixed = mm(agg[...], wt[...], NT)
    hid_ref[...] = jnp.maximum(mixed * width ** (-0.5), 0.0).astype(BF16)
    w_ref[...] = wt[...].astype(F32).T


def swap(x):
    return lax.ppermute(x, "c", [(0, 1), (1, 0)])


def trade(x, axes):
    return lax.all_to_all(x, axes, split_axis=0, concat_axis=0, tiled=True)


def shift(x, axis, distance):
    size = lax.axis_size(axis)
    return lax.ppermute(x, axis, [(i, (i + distance) % size) for i in range(size)])


def spread(x, axis):
    return [x] + [shift(x, axis, step) for step in (1, -1, 2)]


def layer(
    features,
    tile_rows,
    tile_cols,
    tile_vals,
    tile_used,
    pool_weight,
    w_in,
    w_state,
    gate_offset,
    start_weight,
):
    rows_dev, width = features.shape[1:]
    slots = tile_rows.shape[1]
    half = width // 2
    n_tm = lax.axis_size("z")
    feat = features[0]
    blocks_dev = rows_dev // BLOCK

    bf_half = jax.ShapeDtypeStruct((half, width), BF16)
    feat_half = jax.ShapeDtypeStruct((rows_dev, half), BF16)
    send, keep, feat_mine, feat_give = call(
        pool_kernel,
        (bf_half, jax.ShapeDtypeStruct((half, width), F32), pltpu.HBM(feat_half.shape, BF16), feat_half),
        [hspec(), hspec()],
        out=(vspec(), vspec(), hspec(), vspec()),
        scratch=[
            pltpu.VMEM(feat.shape, BF16),
            pltpu.VMEM(pool_weight.shape, BF16),
            pltpu.VMEM(feat_half.shape, BF16),
            pltpu.SemaphoreType.DMA((3,)),
        ],
    )(in_hbm(feat), in_hbm(pool_weight))
    partial = (keep + swap(send).astype(F32)).astype(BF16)
    cols = half // CHIPS
    parts = trade(partial.reshape(CHIPS, cols, width), ("x", "y"))
    snaps = jax.ShapeDtypeStruct((n_tm, cols, width), BF16)
    scale = (rows_dev * CHIPS * C) ** (-0.5)
    summ = call(functools.partial(sum_kernel, scale), snaps, [vspec()], flops=10**7)(parts)
    summ = trade(summ, "z")

    feat_oth = swap(feat_give)
    four = (blocks_dev, BLOCK, half)
    blocks_a = spread(feat_mine.reshape(four), "x")
    blocks_b = spread(feat_oth.reshape(four), "y")
    joined_a, joined_b = join(blocks_a, blocks_b)
    gathered = spread(joined_a, "y") + spread(joined_b, "x")

    w_in_t, w_state_t, start_t, idx_own = call(
        prepare_kernel,
        (pltpu.VMEM(w_in.shape, BF16), pltpu.VMEM(w_state.shape, BF16), pltpu.HBM((cols, width), F32))
        + (jax.ShapeDtypeStruct((2, slots), jnp.int32),),
        [sspec()] * 3 + [hspec()] * 3,
        out=(vspec(), vspec(), hspec(), sspec()),
        scratch=[
            pltpu.VMEM(w_in.shape, BF16),
            pltpu.VMEM(w_state.shape, BF16),
            pltpu.VMEM((width, BLOCK), F32),
            pltpu.VMEM((BLOCK, width), F32),
            pltpu.VMEM((cols, width), F32),
            pltpu.SemaphoreType.DMA((8,)),
        ],
        vmem_mib=12,
    )(tile_rows, tile_cols, tile_used, in_hbm(w_in), in_hbm(w_state), in_hbm(start_weight))
    idx_oth = swap(idx_own)
    tiles_own = tile_vals[0]
    tiles_oth = swap(tiles_own)
    depth = slots * BLOCK
    lhs = pltpu.VMEM((rows_dev, depth), BF16)
    agg_give, rhs_own = call(
        agg_oth_kernel,
        (feat_half, jax.ShapeDtypeStruct((depth, half), BF16)),
        [sspec()] * 2 + [vspec()] * 2 + [pl.BlockSpec(memory_space=pl.ANY)] * len(gathered),
        scratch=[
            pltpu.VMEM((CHIPS * C * blocks_dev, BLOCK, half), BF16),
            pltpu.VMEM((depth, half), BF16),
            lhs,
            pltpu.SemaphoreType.DMA((len(gathered),)),
        ],
        vmem_mib=16,
    )(idx_own, idx_oth, tiles_oth, feat_oth, *gathered)
    agg_oth = swap(agg_give)
    agg_own = call(
        agg_own_kernel, feat_half, [sspec()] + [vspec()] * 3, scratch=[lhs], vmem_mib=8
    )(idx_own, tiles_own, feat_mine, rhs_own)

    evolved = call(
        chain_kernel,
        jax.ShapeDtypeStruct((CHIPS, cols, width), BF16),
        [vspec()] * 4 + [hspec()],
        scratch=[
            pltpu.VMEM((3, n_tm, cols, width), F32),
            pltpu.VMEM((cols, width), F32),
            pltpu.SemaphoreType.DMA(()),
        ],
    )(summ, w_in_t, w_state_t, gate_offset[None, :], start_t)
    wt_own = trade(evolved, ("x", "y")).reshape(half, width)
    wt_oth = swap(wt_own)
    hidden, weights = call(
        final_kernel,
        (jax.ShapeDtypeStruct((rows_dev, width), BF16), jax.ShapeDtypeStruct((width, width), F32)),
        [vspec(), vspec(), vspec(), vspec()],
        scratch=[pltpu.VMEM((width, width), BF16), pltpu.VMEM((rows_dev, width), BF16)],
    )(wt_own, wt_oth, agg_own, agg_oth)
    return hidden[None], weights[None]


def solution(mesh):
    n_tm = mesh.shape["tm"]
    fine = Mesh(mesh.devices.reshape(X, Y, C, n_tm), ("x", "y", "c", "z"))
    dom = ("x", "y", "c")
    in_specs = (
        P("z", dom, None),
        P("z", dom),
        P("z", dom),
        P("z", dom, None, None),
        P("z", dom),
        P(),
        P(),
        P(),
        P(),
        P(),
    )
    out_specs = (P("z", dom, None), P("z", None, None))
    return jax.shard_map(layer, mesh=fine, in_specs=in_specs, out_specs=out_specs, check_vma=False)
```

```python
import functools

import jax
import jax.numpy as jnp
from jax import lax
from jax.experimental import pallas as pl
from jax.experimental.pallas import tpu as pltpu
from jax.sharding import Mesh, PartitionSpec as P


BLOCK = 128
X, Y, C = 4, 4, 2
CHIPS = X * Y
F32 = jnp.float32
BF16 = jnp.bfloat16
VM = pltpu.MemorySpace.VMEM
SM = pltpu.MemorySpace.SMEM
HB = pltpu.MemorySpace.HBM
NN = (((1,), (0,)), ((), ()))
NT = (((1,), (1,)), ((), ()))
TN = (((0,), (0,)), ((), ()))


def mm(a, b, dims):
    return lax.dot_general(a, b, dims, preferred_element_type=F32)


def vspec():
    return pl.BlockSpec(memory_space=VM)


def hspec():
    return pl.BlockSpec(memory_space=HB)


def sspec():
    return pl.BlockSpec(memory_space=SM)


def call(kernel, out_shape, in_specs, scratch=(), flops=10**8, bytes_accessed=10**6, vmem_mib=8, out=None):
    many = isinstance(out_shape, (tuple, list))
    return pl.pallas_call(
        kernel,
        out_shape=out_shape,
        in_specs=in_specs,
        out_specs=out or (tuple(vspec() for _ in out_shape) if many else vspec()),
        scratch_shapes=list(scratch),
        cost_estimate=pl.CostEstimate(flops=flops, bytes_accessed=bytes_accessed, transcendentals=0),
        compiler_params=pltpu.CompilerParams(vmem_limit_bytes=vmem_mib * 2**20),
    )


def place():
    return tuple(lax.axis_index(axis).astype(jnp.int32) for axis in ("x", "y", "c", "z"))


def pool_kernel(
    feat_hbm, pool_hbm, send_ref, keep_ref, mine_hbm, give_ref, feat_ref, pool_ref, mine_ref, sems
):
    fetch = [pltpu.make_async_copy(feat_hbm, feat_ref, sems.at[0]), pltpu.make_async_copy(pool_hbm, pool_ref, sems.at[1])]
    for cp in fetch:
        cp.start()
    for cp in fetch:
        cp.wait()
    half = send_ref.shape[0]
    core = place()[2]
    own = pl.multiple_of(core * half, half)
    other = pl.multiple_of((1 - core) * half, half)
    feat = feat_ref[...]
    gates = jax.nn.sigmoid(mm(feat, pool_ref[:, pl.ds(other, half)], NN)).astype(BF16)
    send_ref[...] = mm(gates, feat, TN).astype(BF16)
    gates = jax.nn.sigmoid(mm(feat, pool_ref[:, pl.ds(own, half)], NN)).astype(BF16)
    mine_ref[...] = feat_ref[:, pl.ds(own, half)]
    give_ref[...] = feat_ref[:, pl.ds(other, half)]
    store = pltpu.make_async_copy(mine_ref, mine_hbm, sems.at[2])
    store.start()
    keep_ref[...] = mm(gates, feat, TN)
    store.wait()


def in_hbm(x):
    return pltpu.with_memory_space_constraint(x, HB)


def join_kernel(*refs):
    n = len(refs) - 4
    pieces, outs, (held, sems) = refs[:n], refs[n : n + 2], refs[n + 2 :]
    half = n // 2
    size = pieces[0].shape[0]

    def fetch(i):
        return pltpu.make_async_copy(pieces[i], held.at[i], sems.at[0, i])

    def store(i):
        return pltpu.make_async_copy(held.at[i], outs[i // half].at[pl.ds((i % half) * size, size)], sems.at[1, i])

    for i in range(n):
        fetch(i).start()
    for i in range(n):
        fetch(i).wait()
        store(i).start()
    for i in range(n):
        store(i).wait()


def join(a, b):
    pieces = a + b
    shape = pltpu.HBM((len(a) * a[0].shape[0],) + a[0].shape[1:], a[0].dtype)
    return call(
        join_kernel,
        (shape, shape),
        [pl.BlockSpec(memory_space=pl.ANY)] * len(pieces),
        out=(hspec(), hspec()),
        scratch=[
            pltpu.VMEM((len(pieces),) + a[0].shape, a[0].dtype),
            pltpu.SemaphoreType.DMA((2, len(pieces))),
        ],
        flops=0,
    )(*pieces)


def sum_kernel(scale, parts_ref, out_ref):
    total = jnp.sum(parts_ref[...].astype(F32), axis=0) * scale
    out_ref[...] = jnp.broadcast_to(total.astype(BF16)[None], out_ref.shape)


def chain_kernel(summ_ref, w_in_ref, w_ref, offset_ref, start_hbm, out_ref, side_ref, startt_ref, start_ref, wt_ref, sem):
    n_t, cols, width = summ_ref.shape
    x, y, core, last = place()
    col0 = core * (width // C) + (x * Y + y) * cols
    window = pl.multiple_of((col0 // BLOCK) * BLOCK, BLOCK)
    fetch = pltpu.make_async_copy(start_hbm.at[:, pl.ds(window, BLOCK)], start_ref, sem)
    fetch.start()
    summ = summ_ref[...].reshape(n_t * cols, width)
    for g in range(3):
        side = mm(summ, w_in_ref[g], NT)
        if g == 0:
            side = side - offset_ref[...]
        side_ref[g] = side.reshape(n_t, cols, width)
    for g in range(3):
        wt_ref[g] = w_ref[g].T
    fetch.wait()
    startt_ref[...] = start_ref[...].T
    state = startt_ref[pl.ds(pl.multiple_of(lax.rem(col0, BLOCK), cols), cols), :]

    def step(t, state):
        state_b = state.astype(BF16)
        reset = jax.nn.sigmoid(side_ref[1, t] + mm(state_b, wt_ref[1], NN))
        update = jax.nn.sigmoid(side_ref[0, t] + mm(state_b, wt_ref[0], NN))
        cand = jnp.tanh(side_ref[2, t] + mm((reset * state).astype(BF16), wt_ref[2], NN))
        return (1.0 - update) * state + update * cand

    state = lax.fori_loop(0, last + 1, step, state)
    out_ref[...] = jnp.broadcast_to(state.astype(BF16)[None], out_ref.shape)


def masked(rows, used, tiles, lhs):
    for j in range(tiles.shape[0]):
        tile = tiles[j]
        at = jnp.where(j < used[0, 0], rows[0, j] & 1, 2)
        for r in range(2):
            lhs[r * BLOCK : (r + 1) * BLOCK, j * BLOCK : (j + 1) * BLOCK] = jnp.where(
                at == r, tile, jnp.zeros_like(tile)
            )


def slot_of(step):
    return jnp.where(step == 0, 0, jnp.where(step == 3, 1, step + 1))


def agg_oth_kernel(cols_own, cols_oth, rows_oth, used_oth, tiles_any, feat_any, *refs):
    pieces, (agg, rhs_own, tiles, feat, blocks, rhs, lhs, sems) = refs[:-8], refs[-8:]
    tile_copy = pltpu.make_async_copy(tiles_any, tiles, sems.at[len(pieces)])
    tile_copy.start()
    feat_copy = pltpu.make_async_copy(feat_any, feat, sems.at[len(pieces) + 1])
    feat_copy.start()
    copies = []
    first = 0
    for n, piece in enumerate(pieces):
        cp = pltpu.make_async_copy(piece, blocks.at[pl.ds(first, piece.shape[0])], sems.at[n])
        cp.start()
        copies.append(cp)
        first += piece.shape[0]
    tile_copy.wait()
    masked(rows_oth, used_oth, tiles, lhs)
    feat_copy.wait()
    for cp in copies:
        cp.wait()
    x, y, core, _ = place()
    for cols, out in ((cols_oth, rhs), (cols_own, rhs_own)):
        for j in range(tiles.shape[0]):
            col = cols[0, j]
            owner = col >> 1
            in_x = slot_of(((owner >> 3) - x) & 3)
            in_y = slot_of(((owner >> 1) - y) & 3)
            slot = jnp.where((owner & 1) == core, in_y * 4 + in_x, in_x * 4 + in_y + CHIPS)
            out[j * BLOCK : (j + 1) * BLOCK, :] = blocks[slot * 2 + (col & 1)]
    agg[...] = (feat[...].astype(F32) + mm(lhs[...], rhs[...], NN)).astype(BF16)


def agg_own_kernel(rows, used, tiles, feat, rhs, agg, lhs):
    masked(rows, used, tiles, lhs)
    agg[...] = (feat[...].astype(F32) + mm(lhs[...], rhs[...], NN)).astype(BF16)


def final_kernel(wt_own, wt_oth, agg_own, agg_oth, hid_ref, w_ref, wt, agg):
    half = wt_own.shape[0]
    core = place()[2]
    own = pl.multiple_of(core * half, half)
    oth = pl.multiple_of((1 - core) * half, half)
    wt[pl.ds(own, half), :] = wt_own[...]
    wt[pl.ds(oth, half), :] = wt_oth[...]
    agg[:, pl.ds(own, half)] = agg_own[...]
    agg[:, pl.ds(oth, half)] = agg_oth[...]
    width = wt.shape[0]
    mixed = mm(agg[...], wt[...], NT)
    hid_ref[...] = jnp.maximum(mixed * width ** (-0.5), 0.0).astype(BF16)
    w_ref[...] = wt[...].astype(F32).T


def swap(x):
    return lax.ppermute(x, "c", [(0, 1), (1, 0)])


def trade(x, axes):
    return lax.all_to_all(x, axes, split_axis=0, concat_axis=0, tiled=True)


def shift(x, axis, distance):
    size = lax.axis_size(axis)
    return lax.ppermute(x, axis, [(i, (i + distance) % size) for i in range(size)])


def spread(x, axis):
    return [x] + [shift(x, axis, step) for step in (1, -1, 2)]


def layer(
    features,
    tile_rows,
    tile_cols,
    tile_vals,
    tile_used,
    pool_weight,
    w_in,
    w_state,
    gate_offset,
    start_weight,
):
    rows_dev, width = features.shape[1:]
    slots = tile_rows.shape[1]
    half = width // 2
    n_tm = lax.axis_size("z")
    feat = features[0]
    blocks_dev = rows_dev // BLOCK

    bf_half = jax.ShapeDtypeStruct((half, width), BF16)
    feat_half = jax.ShapeDtypeStruct((rows_dev, half), BF16)
    send, keep, feat_mine, feat_give = call(
        pool_kernel,
        (bf_half, jax.ShapeDtypeStruct((half, width), F32), pltpu.HBM(feat_half.shape, BF16), feat_half),
        [hspec(), hspec()],
        out=(vspec(), vspec(), hspec(), vspec()),
        scratch=[
            pltpu.VMEM(feat.shape, BF16),
            pltpu.VMEM(pool_weight.shape, BF16),
            pltpu.VMEM(feat_half.shape, BF16),
            pltpu.SemaphoreType.DMA((3,)),
        ],
    )(in_hbm(feat), in_hbm(pool_weight))
    partial = (keep + swap(send).astype(F32)).astype(BF16)
    cols = half // CHIPS
    parts = trade(partial.reshape(CHIPS, cols, width), ("x", "y"))
    snaps = jax.ShapeDtypeStruct((n_tm, cols, width), BF16)
    scale = (rows_dev * CHIPS * C) ** (-0.5)
    summ = call(functools.partial(sum_kernel, scale), snaps, [vspec()], flops=10**7)(parts)
    summ = trade(summ, "z")

    feat_oth = swap(feat_give)
    four = (blocks_dev, BLOCK, half)
    blocks_a = spread(feat_mine.reshape(four), "x")
    blocks_b = spread(feat_oth.reshape(four), "y")
    joined_a, joined_b = join(blocks_a, blocks_b)
    gathered = spread(joined_a, "y") + spread(joined_b, "x")
    gathered = [in_hbm(piece) if piece is joined_a or piece is joined_b else piece for piece in gathered]

    rows_oth, cols_oth, used_oth = swap(tile_rows), swap(tile_cols), swap(tile_used)
    tiles_own = tile_vals[0]
    tiles_oth = swap(tiles_own)
    depth = slots * BLOCK
    lhs = pltpu.VMEM((rows_dev, depth), BF16)
    agg_give, rhs_own = call(
        agg_oth_kernel,
        (feat_half, jax.ShapeDtypeStruct((depth, half), BF16)),
        [sspec()] * 4 + [pl.BlockSpec(memory_space=pl.ANY)] * (len(gathered) + 2),
        scratch=[
            pltpu.VMEM(tiles_oth.shape, BF16),
            pltpu.VMEM(feat_oth.shape, BF16),
            pltpu.VMEM((CHIPS * C * blocks_dev, BLOCK, half), BF16),
            pltpu.VMEM((depth, half), BF16),
            lhs,
            pltpu.SemaphoreType.DMA((len(gathered) + 2,)),
        ],
        vmem_mib=16,
    )(tile_cols, cols_oth, rows_oth, used_oth, tiles_oth, feat_oth, *gathered)
    agg_oth = swap(agg_give)
    agg_own = call(
        agg_own_kernel, feat_half, [sspec()] * 2 + [vspec()] * 3, scratch=[lhs], vmem_mib=8
    )(tile_rows, tile_used, tiles_own, feat_mine, rhs_own)

    evolved = call(
        chain_kernel,
        jax.ShapeDtypeStruct((CHIPS, cols, width), BF16),
        [vspec()] * 4 + [hspec()],
        scratch=[
            pltpu.VMEM((3, n_tm, cols, width), F32),
            pltpu.VMEM((BLOCK, width), F32),
            pltpu.VMEM((width, BLOCK), F32),
            pltpu.VMEM(w_state.shape, BF16),
            pltpu.SemaphoreType.DMA(()),
        ],
        vmem_mib=8,
    )(summ, w_in, w_state, gate_offset[None, :], in_hbm(start_weight))
    wt_own = trade(evolved, ("x", "y")).reshape(half, width)
    wt_oth = swap(wt_own)
    hidden, weights = call(
        final_kernel,
        (jax.ShapeDtypeStruct((rows_dev, width), BF16), jax.ShapeDtypeStruct((width, width), F32)),
        [vspec(), vspec(), vspec(), vspec()],
        scratch=[pltpu.VMEM((width, width), BF16), pltpu.VMEM((rows_dev, width), BF16)],
    )(wt_own, wt_oth, agg_own, agg_oth)
    return hidden[None], weights[None]


def solution(mesh):
    n_tm = mesh.shape["tm"]
    fine = Mesh(mesh.devices.reshape(X, Y, C, n_tm), ("x", "y", "c", "z"))
    dom = ("x", "y", "c")
    in_specs = (
        P("z", dom, None),
        P("z", dom),
        P("z", dom),
        P("z", dom, None, None),
        P("z", dom),
        P(),
        P(),
        P(),
        P(),
        P(),
    )
    out_specs = (P("z", dom, None), P("z", None, None))
    return jax.shard_map(layer, mesh=fine, in_specs=in_specs, out_specs=out_specs, check_vma=False)
```
